32 devices in a mesh: dp: 8 (over z, y), ctx: 4 (over x, core).
Axes of the slice: x: 2, y: 2, z: 4, core: 2. Of those that a mesh axis runs over, the one named last changes fastest.
Arguments:
- tokens: bfloat16 [8, 512, 2048], P('dp', 'ctx'), may hold values from -6 to 6
- segment_ids: int32 [8, 512], P('dp', 'ctx'), may hold values from 0 to 2, as said below
- positions: int32 [8, 512], P('dp', 'ctx'), may hold values from 0 to 511, as said below
- attn_gain: bfloat16 [2048], P(('dp', 'ctx')), may hold values from 0.5 to 1.5
- w_query: bfloat16 [2048, 2048], P(('dp', 'ctx')), may hold values from -0.125 to 0.125
- w_key: bfloat16 [2048, 512], P(('dp', 'ctx')), may hold values from -0.125 to 0.125
- w_value: bfloat16 [2048, 512], P(('dp', 'ctx')), may hold values from -0.125 to 0.125
- w_output: bfloat16 [2048, 2048], P(('dp', 'ctx')), may hold values from -1 to 1
- ffn_gain: bfloat16 [2048], P(('dp', 'ctx')), may hold values from 0.5 to 1.5
- w_gate: bfloat16 [2048, 8192], P('dp', 'ctx'), may hold values from -0.125 to 0.125
- w_up: bfloat16 [2048, 8192], P('dp', 'ctx'), may hold values from -0.125 to 0.125
- w_down: bfloat16 [8192, 2048], P('ctx', 'dp'), may hold values from -0.125 to 0.125
- cotangent: bfloat16 [8, 512, 2048], P('dp', 'ctx'), may hold values from -6 to 6
Outputs:
- mixed: bfloat16 [8, 512, 2048], P('dp', 'ctx')
- grad_tokens: float32 [8, 512, 2048], P('dp', 'ctx')
- grad_attn_gain: float32 [2048], P(('dp', 'ctx'))
- grad_query: float32 [2048, 2048], P(('dp', 'ctx'))
- grad_key: float32 [2048, 512], P(('dp', 'ctx'))
- grad_value: float32 [2048, 512], P(('dp', 'ctx'))
- grad_output: float32 [2048, 2048], P(('dp', 'ctx'))
- grad_ffn_gain: float32 [2048], P(('dp', 'ctx'))
- grad_gate: float32 [2048, 8192], P('dp', 'ctx')
- grad_up: float32 [2048, 8192], P('dp', 'ctx')
- grad_down: float32 [8192, 2048], P('ctx', 'dp')
The draws below stay inside these ranges and needn't reach their ends.
Inputs may be any that keep to these rules, and one draw needn't show every extreme that they name: `segment_ids`: along each packed sequence of 512 tokens the document number never falls and starts at 0; documents do not cross sequences. `positions`: 0 at a document's first token and rising by one along the document; the first packed sequence holds a single document.
All inputs are finite; a program needn't handle non-finite values.
Results may differ from the reference program's by a relative error of at most 0.018.
Values may be sent and summed in bfloat16 or wider, within the bound.
No kernel may reach another device: no remote copies, remote signals or barrier semaphores. Data moves between devices by JAX's collectives and lax.ppermute only.
A program may use at most 256 MiB of HBM per device.

```python
import jax
import jax.numpy as jnp
from jax import lax

D = 2048
QUERY_HEADS = 32
KEY_VALUE_HEADS = 8
HEAD_WIDTH = 64
FF = 8192
PACKED_LENGTH = 512
DOCS = 3
SEQS = 8
QW = 2048
KV_W = 512


def doc_layout(key):
    base = jax.random.fold_in(key, 11)
    cuts = jnp.sort(jax.random.randint(base, (SEQS, DOCS - 1), 1, PACKED_LENGTH), axis=1)
    seq_index = jnp.arange(SEQS, dtype=jnp.int32)
    cuts = jnp.where(seq_index[:, None] == 0, PACKED_LENGTH, cuts).astype(jnp.int32)
    index_row = jnp.arange(PACKED_LENGTH, dtype=jnp.int32)
    passed = (cuts[:, :, None] <= index_row[None, None, :]).astype(jnp.int32)
    segment = jnp.sum(passed, axis=1).astype(jnp.int32)
    starts = jnp.max(jnp.where(passed > 0, cuts[:, :, None], 0), axis=1)
    where_pos = (index_row[None, :] - starts).astype(jnp.int32)
    return (segment, where_pos)


def draw_segment_ids(key, part):
    segment, where_pos = doc_layout(key)
    return segment


def draw_positions(key, part):
    segment, where_pos = doc_layout(key)
    return where_pos


def steps_of(key, extent, cuts, low, largest):
    level = 1.0
    for position, blocks in cuts:
        draws = jax.random.uniform(jax.random.fold_in(jax.random.fold_in(key, 6), position), (blocks,), jnp.float32, low / len(cuts), largest / len(cuts))
        level = level * jnp.repeat(jnp.exp(draws), extent[position] // blocks).reshape((-1,) + (1,) * (len(extent) - 1 - position))
    return level


def noise(stream_key, extent, scale, bound, shards=(), kind=jnp.bfloat16):
    factor_of = steps_of(stream_key, extent, shards, -0.22, 0.18) if shards else 1.0
    entries = jax.random.normal(stream_key, extent, jnp.float32) * scale * factor_of
    return jnp.minimum(jnp.maximum(entries, -bound), bound).astype(kind)


def setup_inputs(seed: int = 0) -> dict:
    keys = jax.random.split(jax.random.key(seed), 14)
    return {
        "tokens": noise(keys[0], (SEQS, PACKED_LENGTH, D), 1.0, 6.0, ((0, 8), (1, 4))),
        "segment_ids": draw_segment_ids(jax.random.fold_in(keys[13], 71), 0),
        "positions": draw_positions(jax.random.fold_in(keys[13], 71), 0),
        "attn_gain": jnp.clip(1.0 + 0.1 * jax.random.normal(keys[3], (D,), jnp.float32), 0.5, 1.5).astype(jnp.bfloat16),
        "w_query": noise(keys[4], (D, QW), D ** -0.5, 0.125, ((0, 32),)),
        "w_key": noise(keys[5], (D, KV_W), D ** -0.5, 0.125, ((0, 32),)),
        "w_value": noise(keys[6], (D, KV_W), D ** -0.5, 0.125, ((0, 32),)),
        "w_output": noise(keys[7], (QW, D), (QW // 64) ** -0.5, 1.0, ((0, 32),)),
        "ffn_gain": jnp.clip(1.0 + 0.1 * jax.random.normal(keys[8], (D,), jnp.float32), 0.5, 1.5).astype(jnp.bfloat16),
        "w_gate": noise(keys[9], (D, FF), D ** -0.5, 0.125, ((0, 8), (1, 4))),
        "w_up": noise(keys[10], (D, FF), D ** -0.5, 0.125, ((0, 8), (1, 4))),
        "w_down": noise(keys[11], (FF, D), (FF // 4) ** -0.5, 0.125, ((0, 4), (1, 8))),
        "cotangent": noise(keys[12], (SEQS, PACKED_LENGTH, D), 1.0, 6.0, ((0, 8), (1, 4))),
    }


EPS_NORM = 1e-05
ROPE_BASE = 500000.0
MASKED = -1e+30

def rope_tables(where_pos, half_width):
    freqs = ROPE_BASE ** (-(jnp.arange(half_width, dtype=jnp.float32) / half_width))
    angles = where_pos.astype(jnp.float32)[..., None] * freqs
    return (jnp.cos(angles), jnp.sin(angles))

def apply_rotation(values, cosine_table, sine_table):
    half_width = values.shape[-1] // 2
    first = values[..., :half_width]
    second = values[..., half_width:]
    cosine_table = cosine_table[..., None, :]
    sine_table = sine_table[..., None, :]
    return jnp.concatenate([first * cosine_table - second * sine_table, second * cosine_table + first * sine_table], axis=-1)

def reverse_rotation(grads, cosine_table, sine_table):
    half_width = grads.shape[-1] // 2
    first = grads[..., :half_width]
    second = grads[..., half_width:]
    cosine_table = cosine_table[..., None, :]
    sine_table = sine_table[..., None, :]
    return jnp.concatenate([first * cosine_table + second * sine_table, second * cosine_table - first * sine_table], axis=-1)

def norm_back(upstream, normed, inverse, gain):
    scaled = upstream * gain
    return inverse * (scaled - normed * lax.optimization_barrier(jnp.mean(scaled * normed, axis=-1, keepdims=True)))

def tdot(left, right):
    return jnp.dot(left.T, right, preferred_element_type=jnp.float32)

def one_sequence(weights, inputs):
    gain_one, wquery, key_weight, value_weight, output_weight, gain_two, wgate, wup_proj, wdown = weights
    tok_rows, seg_row, pos_row, cot_rows = inputs
    query_groups = QUERY_HEADS // KEY_VALUE_HEADS
    factor = 1.0 / HEAD_WIDTH ** 0.5
    gain_onef = gain_one.astype(jnp.float32)
    gain_twof = gain_two.astype(jnp.float32)
    xfloat = tok_rows.astype(jnp.float32)
    inv_one = lax.rsqrt(lax.optimization_barrier(jnp.mean(xfloat * xfloat, axis=-1, keepdims=True)) + EPS_NORM)
    normed_one = xfloat * inv_one
    hidden_first = (normed_one * gain_onef).astype(jnp.bfloat16)
    query_rows = jnp.dot(hidden_first, wquery, preferred_element_type=jnp.float32).reshape(PACKED_LENGTH, QUERY_HEADS, HEAD_WIDTH)
    unrotated_key = jnp.dot(hidden_first, key_weight, preferred_element_type=jnp.float32).reshape(PACKED_LENGTH, KEY_VALUE_HEADS, HEAD_WIDTH)
    value_second = jnp.dot(hidden_first, value_weight, preferred_element_type=jnp.float32).astype(jnp.bfloat16).reshape(PACKED_LENGTH, KEY_VALUE_HEADS, HEAD_WIDTH)
    cosine_table, sine_table = rope_tables(pos_row, HEAD_WIDTH // 2)
    rotated_query = apply_rotation(query_rows, cosine_table, sine_table).astype(jnp.bfloat16).reshape(PACKED_LENGTH, KEY_VALUE_HEADS, query_groups, HEAD_WIDTH)
    rkey = apply_rotation(unrotated_key, cosine_table, sine_table).astype(jnp.bfloat16)
    index_row = jnp.arange(PACKED_LENGTH, dtype=jnp.int32)
    allowed = (seg_row[:, None] == seg_row[None, :]) & (index_row[None, :] <= index_row[:, None])
    scores = jnp.einsum('chgd,lhd->hgcl', rotated_query.astype(jnp.float32), rkey.astype(jnp.float32)) * factor
    masked = jnp.where(allowed, scores, MASKED)
    expo = jnp.exp(masked)
    total = lax.optimization_barrier(jnp.sum(expo, axis=-1, keepdims=True))
    lse = jnp.log(total)
    probs = (expo / total).astype(jnp.bfloat16)
    attended = jnp.einsum('hgcl,lhd->chgd', probs.astype(jnp.float32), value_second.astype(jnp.float32))
    attended = attended.astype(jnp.bfloat16).reshape(PACKED_LENGTH, QW)
    resid = xfloat + jnp.dot(attended, output_weight, preferred_element_type=jnp.float32)
    inv_two = lax.rsqrt(lax.optimization_barrier(jnp.mean(resid * resid, axis=-1, keepdims=True)) + EPS_NORM)
    normed_two = resid * inv_two
    h_two = (normed_two * gain_twof).astype(jnp.bfloat16)
    gate = jnp.dot(h_two, wgate, preferred_element_type=jnp.float32)
    up_proj = jnp.dot(h_two, wup_proj, preferred_element_type=jnp.float32)
    sigma = jax.nn.sigmoid(gate)
    hidden = (gate * sigma * up_proj).astype(jnp.bfloat16)
    mixed = (resid + jnp.dot(hidden, wdown, preferred_element_type=jnp.float32)).astype(jnp.bfloat16)
    cot_float = cot_rows.astype(jnp.float32)
    d_hidden = jnp.dot(cot_rows, wdown.T, preferred_element_type=jnp.float32)
    grad_down = tdot(hidden, cot_rows)
    d_up = (d_hidden * gate * sigma).astype(jnp.bfloat16)
    d_gate = (d_hidden * up_proj * sigma * (1.0 + gate * (1.0 - sigma))).astype(jnp.bfloat16)
    grad_gate = tdot(h_two, d_gate)
    grad_up = tdot(h_two, d_up)
    d_h_two = jnp.dot(d_gate, wgate.T, preferred_element_type=jnp.float32) + jnp.dot(d_up, wup_proj.T, preferred_element_type=jnp.float32)
    grad_gain_two = lax.optimization_barrier(jnp.sum(d_h_two * normed_two, axis=0))
    d_resid = cot_float + norm_back(d_h_two, normed_two, inv_two, gain_twof)
    residual_gradient_second = d_resid.astype(jnp.bfloat16)
    grad_output = tdot(attended, residual_gradient_second)
    attended_gradient = jnp.dot(residual_gradient_second, output_weight.T, preferred_element_type=jnp.float32).astype(jnp.bfloat16).reshape(PACKED_LENGTH, KEY_VALUE_HEADS, query_groups, HEAD_WIDTH)
    probs_f = jnp.where(allowed, jnp.exp(masked - lse), 0.0)
    d_probs = jnp.einsum('chgd,lhd->hgcl', attended_gradient.astype(jnp.float32), value_second.astype(jnp.float32))
    delta = lax.optimization_barrier(jnp.sum(probs_f * d_probs, axis=-1, keepdims=True))
    d_scores = probs_f * (d_probs - delta)
    value_gradient_local = jnp.einsum('hgcl,chgd->lhd', probs_f.astype(jnp.bfloat16).astype(jnp.float32), attended_gradient.astype(jnp.float32))
    d_scores_b = (d_scores * factor).astype(jnp.bfloat16).astype(jnp.float32)
    d_rquery = jnp.einsum('hgcl,lhd->chgd', d_scores_b, rkey.astype(jnp.float32)).reshape(PACKED_LENGTH, QUERY_HEADS, HEAD_WIDTH)
    rotated_key_gradient = jnp.einsum('hgcl,chgd->lhd', d_scores_b, rotated_query.astype(jnp.float32))
    dquery = reverse_rotation(d_rquery, cosine_table, sine_table).astype(jnp.bfloat16).reshape(PACKED_LENGTH, QW)
    dkey = reverse_rotation(rotated_key_gradient, cosine_table, sine_table).astype(jnp.bfloat16).reshape(PACKED_LENGTH, KV_W)
    value_gradient_full = value_gradient_local.astype(jnp.bfloat16).reshape(PACKED_LENGTH, KV_W)
    grad_query = tdot(hidden_first, dquery)
    grad_key = tdot(hidden_first, dkey)
    grad_value = tdot(hidden_first, value_gradient_full)
    d_h_one = jnp.dot(dquery, wquery.T, preferred_element_type=jnp.float32)
    d_h_one = d_h_one + jnp.dot(dkey, key_weight.T, preferred_element_type=jnp.float32)
    d_h_one = d_h_one + jnp.dot(value_gradient_full, value_weight.T, preferred_element_type=jnp.float32)
    grad_gain_one = lax.optimization_barrier(jnp.sum(d_h_one * normed_one, axis=0))
    grad_tokens = d_resid + norm_back(d_h_one, normed_one, inv_one, gain_onef)
    grads = (grad_gain_one, grad_query, grad_key, grad_value, grad_output, grad_gain_two, grad_gate, grad_up, grad_down)
    return (mixed, grad_tokens, grads)

def reference(tokens, segment_ids, positions, attn_gain, w_query, w_key, w_value, w_output, ffn_gain, w_gate, w_up, w_down, cotangent):
    weights = (attn_gain, w_query, w_key, w_value, w_output, ffn_gain, w_gate, w_up, w_down)
    zeros = (jnp.zeros((D,), jnp.float32), jnp.zeros((D, QW), jnp.float32), jnp.zeros((D, KV_W), jnp.float32), jnp.zeros((D, KV_W), jnp.float32), jnp.zeros((QW, D), jnp.float32), jnp.zeros((D,), jnp.float32), jnp.zeros((D, FF), jnp.float32), jnp.zeros((D, FF), jnp.float32), jnp.zeros((FF, D), jnp.float32))

    def step_fn(carry, inputs):
        mixed, grad_tokens, grads = one_sequence(weights, inputs)
        carry = tuple((left + right for left, right in zip(carry, grads)))
        return (carry, (mixed, grad_tokens))
    sums, outputs = lax.scan(step_fn, zeros, (tokens, segment_ids, positions, cotangent))
    mixed, grad_tokens = outputs
    return (mixed, grad_tokens, sums[0], sums[1], sums[2], sums[3], sums[4], sums[5], sums[6], sums[7], sums[8])
```

```python
import jax
import jax.numpy as jnp
from jax import lax
from jax.sharding import Mesh
from jax.sharding import PartitionSpec as P

QUERY_HEADS = 32
KEY_VALUE_HEADS = 8
HEAD_WIDTH = 64


EPS_NORM = 1e-05
ROPE_BASE = 500000.0
MASKED = -1e30


F32 = jnp.float32
BF16 = jnp.bfloat16


def rope_tables(where_pos, half_width):
    freqs = ROPE_BASE ** (-(jnp.arange(half_width, dtype=jnp.float32) / half_width))
    angles = where_pos.astype(jnp.float32)[..., None] * freqs
    return (jnp.cos(angles), jnp.sin(angles))


def apply_rotation(values, cosine_table, sine_table):
    half_width = values.shape[-1] // 2
    first = values[..., :half_width]
    second = values[..., half_width:]
    cosine_table = cosine_table[..., None, :]
    sine_table = sine_table[..., None, :]
    return jnp.concatenate(
        [first * cosine_table - second * sine_table, second * cosine_table + first * sine_table],
        axis=-1,
    )


def reverse_rotation(grads, cosine_table, sine_table):
    half_width = grads.shape[-1] // 2
    first = grads[..., :half_width]
    second = grads[..., half_width:]
    cosine_table = cosine_table[..., None, :]
    sine_table = sine_table[..., None, :]
    return jnp.concatenate(
        [first * cosine_table + second * sine_table, second * cosine_table - first * sine_table],
        axis=-1,
    )


def norm_back(upstream, normed, inverse, gain):
    scaled = upstream * gain
    return inverse * (scaled - normed * jnp.mean(scaled * normed, axis=-1, keepdims=True))


def tdot(left, right):
    return lax.dot_general(
        left, right, (((0,), (0,)), ((), ())), preferred_element_type=jnp.float32
    )


def dot_t(left, right):
    return lax.dot_general(
        left, right, (((1,), (1,)), ((), ())), preferred_element_type=jnp.float32
    )


def shift(value, axis, step=1):
    count = lax.axis_size(axis)
    return lax.ppermute(value, axis, [(i, (i + step) % count) for i in range(count)])


def gather_ring(value, axis):
    slots = [value]
    for _ in range(lax.axis_size(axis) - 1):
        slots.append(shift(slots[-1], axis))
    return slots


def add_rounded(left, right):
    return (left.astype(F32) + right.astype(F32)).astype(left.dtype)


def reduce_ring(parts, axis):
    count = lax.axis_size(axis)
    if count == 1:
        return parts[0]
    total = parts[1]
    for k in range(2, count):
        total = add_rounded(shift(total, axis), parts[k])
    return add_rounded(shift(total, axis), parts[0])


def gather_tokens(value):
    slots = []
    for piece in gather_ring(value, "z"):
        pair = jnp.concatenate(gather_ring(piece, "x"), axis=0)
        slots.append(jnp.concatenate(gather_ring(pair, "c"), axis=0))
    return slots


def reduce_block(block):
    cores = lax.axis_size("c")
    across = lax.axis_size("x")
    rows = block.shape[0] // cores
    pair = reduce_ring([block[k * rows : (k + 1) * rows] for k in range(cores)], "c")
    rows = rows // across
    return reduce_ring([pair[k * rows : (k + 1) * rows] for k in range(across)], "x")


def reduce_tokens(blocks):
    count = len(blocks)
    order = [k % count for k in range(1, count + 1)]
    local = {k: reduce_block(blocks[k]) for k in order}
    return reduce_ring([local[k] for k in range(count)], "z")


def reduce_rows(block):
    cores, along_y, along_x = block.shape[:3]
    own = reduce_ring([block[k] for k in range(cores)], "c")
    half = own.shape[-1] // 2
    left, right = own[..., :half], own[..., half:]
    left = reduce_ring([left[k] for k in range(along_y)], "y")
    left = reduce_ring([left[k] for k in range(along_x)], "x")
    right = reduce_ring([right[:, k] for k in range(along_x)], "x")
    right = reduce_ring([right[k] for k in range(along_y)], "y")
    return jnp.concatenate([left, right], axis=-1)


def reduce_weight(permuted, upstream, shape):
    count = lax.axis_size("z")
    columns = permuted.shape[1] // count
    local = {}
    for step in range(1, count + 1):
        k = step % count
        part = tdot(permuted[:, k * columns : (k + 1) * columns], upstream).astype(BF16)
        local[k] = reduce_rows(part.reshape(shape + part.shape[1:]))
    return reduce_ring([local[k] for k in range(count)], "z")


def gather_small(value):
    value = jnp.concatenate(gather_ring(value, "x"), axis=0)
    value = jnp.concatenate(gather_ring(value, "y"), axis=0)
    value = jnp.concatenate(gather_ring(value, "c"), axis=0)
    return jnp.concatenate(gather_ring(value, "z"), axis=0)


def reduce_small(value):
    for axis in ("z", "c", "y", "x"):
        count = lax.axis_size(axis)
        value = value.reshape((count, value.shape[0] // count) + value.shape[1:])
        value = reduce_ring([value[k] for k in range(count)], axis)
    return value


def body(
    tokens,
    segment_ids,
    positions,
    attn_gain,
    w_query,
    w_key,
    w_value,
    w_output,
    ffn_gain,
    w_gate,
    w_up,
    w_down,
    cotangent,
):
    everywhere = ("z", "y", "x", "c")
    size_z, size_y, size_x, size_c = (lax.axis_size(a) for a in everywhere)
    at_z, at_y, at_x, at_c = (lax.axis_index(a) for a in everywhere)
    devices = size_z * size_y * size_x * size_c
    count_ctx = size_x * size_c
    local_sequence, context_rows, width = tokens.shape
    token_rows = local_sequence * context_rows
    sequence_length = context_rows * count_ctx
    query_groups = QUERY_HEADS // KEY_VALUE_HEADS
    query_width = QUERY_HEADS * HEAD_WIDTH
    kv_width = KEY_VALUE_HEADS * HEAD_WIDTH
    factor = 1.0 / HEAD_WIDTH**0.5
    own_rows = w_query.shape[0]

    distance = jnp.arange(devices, dtype=jnp.int32)
    dist_x = distance % size_x
    dist_y = (distance // size_x) % size_y
    dist_c = (distance // (size_x * size_y)) % size_c
    dist_z = distance // (size_x * size_y * size_c)
    piece = ((at_z - dist_z) % size_z) * size_y + (at_y - dist_y) % size_y
    piece = piece * size_x + (at_x - dist_x) % size_x
    piece = piece * size_c + (at_c - dist_c) % size_c
    feature = (piece[:, None] * own_rows + jnp.arange(own_rows, dtype=jnp.int32)).reshape(-1)
    selector = (jnp.arange(width, dtype=jnp.int32)[:, None] == feature[None, :]).astype(BF16)

    def by_distance(value):
        return jnp.dot(value, selector, preferred_element_type=F32).astype(BF16)

    qkv_weight = lax.all_gather(
        jnp.concatenate([w_query, w_key, w_value], axis=1), everywhere, axis=0, tiled=True
    )
    output_weight = lax.all_gather(w_output, everywhere, axis=0, tiled=True)
    gains = gather_small(jnp.stack([attn_gain, ffn_gain])[None].astype(F32))
    place = jnp.argmax(
        (piece[None, :] == distance[:, None]).astype(jnp.int32), axis=1
    )
    gains = jnp.take(gains, place, axis=0)
    gain_onef = gains[:, 0].reshape(width)
    gain_twof = gains[:, 1].reshape(width)

    ff_width = w_gate.shape[1]
    ff_own = ff_width // size_z
    ff_rows = w_gate.shape[0]
    w_down_t = w_down.T

    def hidden_block(which):
        start = which * ff_own
        return jnp.concatenate(
            [
                lax.dynamic_slice_in_dim(w_gate, start, ff_own, axis=1),
                lax.dynamic_slice_in_dim(w_up, start, ff_own, axis=1),
                lax.dynamic_slice_in_dim(w_down_t, start, ff_own, axis=1),
            ],
            axis=1,
        )

    ffn = jnp.zeros((width, 3 * ff_own), BF16)
    for step in range(size_z):
        block = hidden_block((at_z + step) % size_z)
        if step:
            block = shift(block, "z", step)
        for k, piece_y in enumerate(gather_ring(block, "y")):
            row = ((at_z - step) % size_z) * size_y + (at_y - k) % size_y
            ffn = lax.dynamic_update_slice_in_dim(ffn, piece_y, row * ff_rows, axis=0)
    gate_up_weight = ffn[:, : 2 * ff_own]
    down_weight_t = ffn[:, 2 * ff_own :]
    cot_slots = gather_tokens(cotangent.reshape(token_rows, width))

    xfloat = tokens.reshape(token_rows, width).astype(F32)
    inv_one = lax.rsqrt(jnp.mean(xfloat * xfloat, axis=-1, keepdims=True) + EPS_NORM)
    normed_one = xfloat * inv_one
    hidden_first = (normed_one * gain_onef).astype(BF16)
    qkv = jnp.dot(hidden_first, qkv_weight, preferred_element_type=F32)
    query_rows = qkv[:, :query_width].reshape(
        local_sequence, context_rows, QUERY_HEADS, HEAD_WIDTH
    )
    unrotated_key = qkv[:, query_width : query_width + kv_width].reshape(
        local_sequence, context_rows, KEY_VALUE_HEADS, HEAD_WIDTH
    )
    value_own = (
        qkv[:, query_width + kv_width :].astype(BF16).reshape(local_sequence, context_rows, kv_width)
    )
    cosine_table, sine_table = rope_tables(positions, HEAD_WIDTH // 2)
    rotated_query = (
        apply_rotation(query_rows, cosine_table, sine_table)
        .astype(BF16)
        .reshape(local_sequence, context_rows, KEY_VALUE_HEADS, query_groups, HEAD_WIDTH)
    )
    rkey_own = (
        apply_rotation(unrotated_key, cosine_table, sine_table)
        .astype(BF16)
        .reshape(local_sequence, context_rows, kv_width)
    )

    def gather_sequence(value):
        value = jnp.concatenate(gather_ring(value, "x"), axis=1)
        return jnp.concatenate(gather_ring(value, "c"), axis=1)

    at_ctx = at_x * size_c + at_c
    query_index = at_ctx * context_rows + jnp.arange(context_rows, dtype=jnp.int32)
    slot = jnp.arange(count_ctx, dtype=jnp.int32)
    slot_ctx = ((at_x - slot % size_x) % size_x) * size_c + (at_c - slot // size_x) % size_c
    key_index = (
        slot_ctx[:, None] * context_rows + jnp.arange(context_rows, dtype=jnp.int32)[None, :]
    ).reshape(-1)
    segments_all = gather_sequence(segment_ids)
    allowed = (segment_ids[:, :, None] == segments_all[:, None, :]) & (
        key_index[None, None, :] <= query_index[None, :, None]
    )
    allowed = allowed[:, None, None]
    gathered = gather_sequence(jnp.concatenate([rkey_own, value_own], axis=-1))
    gathered_keys = gathered[..., :kv_width].reshape(
        local_sequence, sequence_length, KEY_VALUE_HEADS, HEAD_WIDTH
    )
    gathered_values = gathered[..., kv_width:].reshape(
        local_sequence, sequence_length, KEY_VALUE_HEADS, HEAD_WIDTH
    )
    scores = (
        jnp.einsum("schgd,slhd->shgcl", rotated_query, gathered_keys, preferred_element_type=F32)
        * factor
    )
    masked = jnp.where(allowed, scores, MASKED)
    expo = jnp.exp(masked)
    total = jnp.sum(expo, axis=-1, keepdims=True)
    lse = jnp.log(total)
    probs = (expo / total).astype(BF16)
    attended = jnp.einsum("shgcl,slhd->schgd", probs, gathered_values, preferred_element_type=F32)
    attended = attended.astype(BF16).reshape(token_rows, query_width)
    resid = xfloat + jnp.dot(attended, output_weight, preferred_element_type=F32)
    inv_two = lax.rsqrt(jnp.mean(resid * resid, axis=-1, keepdims=True) + EPS_NORM)
    normed_two = resid * inv_two
    h_two = (normed_two * gain_twof).astype(BF16)

    h_slots = gather_tokens(h_two)
    hidden_slots, d_slots, out_slots, d_h_slots = [], [], [], []
    for h_slot, cot_slot in zip(h_slots, cot_slots):
        gate_up = jnp.dot(h_slot, gate_up_weight, preferred_element_type=F32)
        gate, up_proj = gate_up[:, :ff_own], gate_up[:, ff_own:]
        sigma = jax.nn.sigmoid(gate)
        hidden = (gate * sigma * up_proj).astype(BF16)
        d_hidden = jnp.dot(cot_slot, down_weight_t, preferred_element_type=F32)
        d_up = (d_hidden * gate * sigma).astype(BF16)
        d_gate = (d_hidden * up_proj * sigma * (1.0 + gate * (1.0 - sigma))).astype(BF16)
        d_both = jnp.concatenate([d_gate, d_up], axis=1)
        d_h_slots.append(dot_t(d_both, gate_up_weight).astype(BF16))
        out_slots.append(dot_t(hidden, down_weight_t).astype(BF16))
        hidden_slots.append(hidden)
        d_slots.append(d_both)
    d_h_two = reduce_tokens(d_h_slots).astype(F32)
    ffn_out = reduce_tokens(out_slots).astype(F32)
    mixed = (resid + ffn_out).astype(BF16)

    h_all = jnp.concatenate(h_slots, axis=0)
    cot_all = jnp.concatenate(cot_slots, axis=0)
    grad_ffn = jnp.concatenate(
        [
            tdot(h_all, jnp.concatenate(d_slots, axis=0)).astype(BF16),
            tdot(cot_all, jnp.concatenate(hidden_slots, axis=0)).astype(BF16),
        ],
        axis=1,
    )
    grad_gate = jnp.zeros((ff_rows, ff_width), F32)
    grad_up = jnp.zeros((ff_rows, ff_width), F32)
    grad_down_t = jnp.zeros((ff_rows, ff_width), F32)
    for step in range(size_z):
        rows_y = []
        for k in range(size_y):
            row = ((at_z - step) % size_z) * size_y + (at_y - k) % size_y
            rows_y.append(lax.dynamic_slice_in_dim(grad_ffn, row * ff_rows, ff_rows, axis=0))
        block = reduce_ring(rows_y, "y")
        if step:
            block = shift(block, "z", -step)
        start = ((at_z + step) % size_z) * ff_own
        block = block.astype(F32)
        grad_gate = lax.dynamic_update_slice_in_dim(grad_gate, block[:, :ff_own], start, axis=1)
        grad_up = lax.dynamic_update_slice_in_dim(
            grad_up, block[:, ff_own : 2 * ff_own], start, axis=1
        )
        grad_down_t = lax.dynamic_update_slice_in_dim(
            grad_down_t, block[:, 2 * ff_own :], start, axis=1
        )
    grad_down = grad_down_t.T

    gain_term_two = jnp.sum(d_h_two * normed_two, axis=0)
    cot_rows = cotangent.reshape(token_rows, width)
    d_resid = cot_rows.astype(F32) + norm_back(d_h_two, normed_two, inv_two, gain_twof)
    residual_gradient_second = d_resid.astype(BF16)
    attended_gradient = dot_t(residual_gradient_second, output_weight).astype(BF16)
    attended_gradient = attended_gradient.reshape(
        local_sequence, context_rows, KEY_VALUE_HEADS, query_groups, HEAD_WIDTH
    )
    shape = (size_c, size_y, size_x, own_rows)
    grad_output = reduce_weight(by_distance(attended), residual_gradient_second, shape).astype(F32)
    probs_f = jnp.where(allowed, jnp.exp(masked - lse), 0.0)
    d_probs = jnp.einsum(
        "schgd,slhd->shgcl", attended_gradient, gathered_values, preferred_element_type=F32
    )
    delta = jnp.sum(probs_f * d_probs, axis=-1, keepdims=True)
    d_scores_b = (probs_f * (d_probs - delta) * factor).astype(BF16)
    value_gradient_local = jnp.einsum(
        "shgcl,schgd->slhd",
        probs_f.astype(BF16),
        attended_gradient,
        preferred_element_type=F32,
    )
    d_rquery = jnp.einsum(
        "shgcl,slhd->schgd", d_scores_b, gathered_keys, preferred_element_type=F32
    )
    rotated_key_gradient = jnp.einsum(
        "shgcl,schgd->slhd", d_scores_b, rotated_query, preferred_element_type=F32
    )
    kv_gradient = jnp.concatenate(
        [
            rotated_key_gradient.reshape(local_sequence, sequence_length, kv_width).astype(BF16),
            value_gradient_local.reshape(local_sequence, sequence_length, kv_width).astype(BF16),
        ],
        axis=-1,
    )
    for axis in ("c", "x"):
        count = lax.axis_size(axis)
        kv_gradient = reduce_ring(jnp.split(kv_gradient, count, axis=1), axis)
    kv_gradient = kv_gradient.astype(F32)
    dquery = (
        reverse_rotation(
            d_rquery.reshape(local_sequence, context_rows, QUERY_HEADS, HEAD_WIDTH),
            cosine_table,
            sine_table,
        )
        .astype(BF16)
        .reshape(token_rows, query_width)
    )
    dkey = (
        reverse_rotation(
            kv_gradient[..., :kv_width].reshape(
                local_sequence, context_rows, KEY_VALUE_HEADS, HEAD_WIDTH
            ),
            cosine_table,
            sine_table,
        )
        .astype(BF16)
        .reshape(token_rows, kv_width)
    )
    dvalue = kv_gradient[..., kv_width:].astype(BF16).reshape(token_rows, kv_width)
    d_qkv = jnp.concatenate([dquery, dkey, dvalue], axis=1)
    grad_qkv = reduce_weight(by_distance(hidden_first), d_qkv, shape).astype(F32)
    d_h_one = dot_t(d_qkv, qkv_weight)
    gain_term_one = jnp.sum(d_h_one * normed_one, axis=0)
    grad_tokens = d_resid + norm_back(d_h_one, normed_one, inv_one, gain_onef)
    gain_terms = jnp.stack(
        [gain_term_one.reshape(devices, own_rows), gain_term_two.reshape(devices, own_rows)], axis=1
    )
    gain_grads = reduce_small(jnp.take(gain_terms, piece, axis=0))[0]
    return (
        mixed.reshape(local_sequence, context_rows, width),
        grad_tokens.reshape(local_sequence, context_rows, width),
        gain_grads[0],
        grad_qkv[:, :query_width],
        grad_qkv[:, query_width : query_width + kv_width],
        grad_qkv[:, query_width + kv_width :],
        grad_output,
        gain_grads[1],
        grad_gate,
        grad_up,
        grad_down,
    )


def solution(mesh):
    count_dp, count_ctx = mesh.devices.shape
    along_z = 4 if count_dp % 4 == 0 else count_dp
    along_x = 2 if count_ctx % 2 == 0 else 1
    fine = Mesh(
        mesh.devices.reshape(along_z, count_dp // along_z, along_x, count_ctx // along_x),
        ("z", "y", "x", "c"),
    )
    dp, ctx, both = ("z", "y"), ("x", "c"), ("z", "y", "x", "c")
    return jax.shard_map(
        body,
        mesh=fine,
        in_specs=(
            P(dp, ctx, None),
            P(dp, ctx),
            P(dp, ctx),
            P(both),
            P(both, None),
            P(both, None),
            P(both, None),
            P(both, None),
            P(both),
            P(dp, ctx),
            P(dp, ctx),
            P(ctx, dp),
            P(dp, ctx, None),
        ),
        out_specs=(
            P(dp, ctx, None),
            P(dp, ctx, None),
            P(both),
            P(both, None),
            P(both, None),
            P(both, None),
            P(both, None),
            P(both),
            P(dp, ctx),
            P(dp, ctx),
            P(ctx, dp),
        ),
        check_vma=False,
    )
```

```python
import jax
import jax.numpy as jnp
from jax import lax
from jax.sharding import Mesh
from jax.sharding import PartitionSpec as P

QUERY_HEADS = 32
KEY_VALUE_HEADS = 8
HEAD_WIDTH = 64


EPS_NORM = 1e-05
ROPE_BASE = 500000.0
MASKED = -1e30


F32 = jnp.float32
BF16 = jnp.bfloat16


def rope_tables(where_pos, half_width):
    freqs = ROPE_BASE ** (-(jnp.arange(half_width, dtype=jnp.float32) / half_width))
    angles = where_pos.astype(jnp.float32)[..., None] * freqs
    return (jnp.cos(angles), jnp.sin(angles))


def apply_rotation(values, cosine_table, sine_table):
    half_width = values.shape[-1] // 2
    first = values[..., :half_width]
    second = values[..., half_width:]
    cosine_table = cosine_table[..., None, :]
    sine_table = sine_table[..., None, :]
    return jnp.concatenate(
        [first * cosine_table - second * sine_table, second * cosine_table + first * sine_table],
        axis=-1,
    )


def reverse_rotation(grads, cosine_table, sine_table):
    half_width = grads.shape[-1] // 2
    first = grads[..., :half_width]
    second = grads[..., half_width:]
    cosine_table = cosine_table[..., None, :]
    sine_table = sine_table[..., None, :]
    return jnp.concatenate(
        [first * cosine_table + second * sine_table, second * cosine_table - first * sine_table],
        axis=-1,
    )


def norm_back(upstream, normed, inverse, gain):
    scaled = upstream * gain
    return inverse * (scaled - normed * jnp.mean(scaled * normed, axis=-1, keepdims=True))


def tdot(left, right):
    return lax.dot_general(
        left, right, (((0,), (0,)), ((), ())), preferred_element_type=jnp.float32
    )


def dot_t(left, right):
    return lax.dot_general(
        left, right, (((1,), (1,)), ((), ())), preferred_element_type=jnp.float32
    )


def shift(value, axis, step=1):
    count = lax.axis_size(axis)
    return lax.ppermute(value, axis, [(i, (i + step) % count) for i in range(count)])


def gather_ring(value, axis):
    slots = [value]
    for _ in range(lax.axis_size(axis) - 1):
        slots.append(shift(slots[-1], axis))
    return slots


def add_rounded(left, right):
    return (left.astype(F32) + right.astype(F32)).astype(left.dtype)


def reduce_ring(parts, axis):
    count = lax.axis_size(axis)
    if count == 1:
        return parts[0]
    total = parts[1]
    for k in range(2, count):
        total = add_rounded(shift(total, axis), parts[k])
    return add_rounded(shift(total, axis), parts[0])


def gather_tokens(value):
    slots = []
    for piece in gather_ring(value, "z"):
        pair = jnp.concatenate(gather_ring(piece, "x"), axis=0)
        slots.append(jnp.concatenate(gather_ring(pair, "c"), axis=0))
    return slots


def reduce_block(block):
    cores = lax.axis_size("c")
    across = lax.axis_size("x")
    rows = block.shape[0] // cores
    pair = reduce_ring([block[k * rows : (k + 1) * rows] for k in range(cores)], "c")
    rows = rows // across
    return reduce_ring([pair[k * rows : (k + 1) * rows] for k in range(across)], "x")


def reduce_locally(blocks):
    count = len(blocks)
    local = {k % count: reduce_block(blocks[k % count]) for k in range(1, count + 1)}
    return [local[k] for k in range(count)]


def hop_order(slot):
    return ("y", "x", "c") if slot % 2 == 0 else ("x", "y", "c")


def gather_rows(piece, slot):
    for axis in hop_order(slot):
        piece = jnp.concatenate(gather_ring(piece, axis), axis=0)
    return piece


def reduce_axes(block, axes):
    for axis in axes:
        rows = block.shape[-2] // lax.axis_size(axis)
        parts = [block[..., k * rows : (k + 1) * rows, :] for k in range(lax.axis_size(axis))]
        block = reduce_ring(parts, axis)
    return block


def reduce_weight(permuted, upstream):
    count = lax.axis_size("z")
    columns = permuted.shape[1] // count
    local = {}
    for step in range(1, count + 1):
        k = step % count
        part = tdot(permuted[:, k * columns : (k + 1) * columns], upstream).astype(BF16)
        local[k] = reduce_axes(part, reversed(hop_order(k)))
    local = [local[k] for k in range(count)]
    return reduce_ring(local, "z"), local


def rows_product(value, slots):
    rows = slots[0].shape[0]
    total = None
    for k, slot in enumerate(slots):
        part = jnp.dot(value[:, k * rows : (k + 1) * rows], slot, preferred_element_type=F32)
        total = part if total is None else total + part
    return total


def after(values, *waits):
    return lax.optimization_barrier((tuple(values), waits))[0]


def reduce_small(value):
    for axis in ("c", "x", "y", "z"):
        count = lax.axis_size(axis)
        value = value.reshape((count, value.shape[0] // count) + value.shape[1:])
        value = reduce_ring([value[k] for k in range(count)], axis)
    return value


def body(
    tokens,
    segment_ids,
    positions,
    attn_gain,
    w_query,
    w_key,
    w_value,
    w_output,
    ffn_gain,
    w_gate,
    w_up,
    w_down,
    cotangent,
):
    everywhere = ("z", "y", "x", "c")
    size_z, size_y, size_x, size_c = (lax.axis_size(a) for a in everywhere)
    at_z, at_y, at_x, at_c = (lax.axis_index(a) for a in everywhere)
    devices = size_z * size_y * size_x * size_c
    count_ctx = size_x * size_c
    local_sequence, context_rows, width = tokens.shape
    token_rows = local_sequence * context_rows
    sequence_length = context_rows * count_ctx
    query_groups = QUERY_HEADS // KEY_VALUE_HEADS
    query_width = QUERY_HEADS * HEAD_WIDTH
    kv_width = KEY_VALUE_HEADS * HEAD_WIDTH
    factor = 1.0 / HEAD_WIDTH**0.5
    own_rows = w_query.shape[0]

    sizes = {"y": size_y, "x": size_x, "c": size_c}
    here = {"y": at_y, "x": at_x, "c": at_c}
    plane = jnp.arange(devices // size_z, dtype=jnp.int32)
    pieces = []
    for slot in range(size_z):
        stride, at = 1, {}
        for axis in hop_order(slot):
            away = (plane // stride) % sizes[axis]
            at[axis] = (here[axis] - away) % sizes[axis]
            stride *= sizes[axis]
        row = ((at_z - slot) % size_z) * size_y + at["y"]
        pieces.append((row * size_x + at["x"]) * size_c + at["c"])
    piece = jnp.concatenate(pieces)
    feature = (piece[:, None] * own_rows + jnp.arange(own_rows, dtype=jnp.int32)).reshape(-1)
    selector = (jnp.arange(width, dtype=jnp.int32)[:, None] == feature[None, :]).astype(BF16)

    def by_distance(value):
        return jnp.dot(value, selector, preferred_element_type=F32).astype(BF16)

    def by_feature(value):
        return dot_t(value.astype(BF16), selector)

    with jax.named_scope("gather_gains"):
        gains = jnp.concatenate(
            gather_ring(jnp.stack([attn_gain, ffn_gain])[None].astype(F32), "z"), axis=0
        )
    with jax.named_scope("gather_qkv"):
        qkv_own = jnp.concatenate([w_query, w_key, w_value], axis=1)
        gains_z = gains
        (qkv_sent,) = after((qkv_own,), gains_z)
        qkv_ring = [qkv_own] + gather_ring(qkv_sent, "z")[1:]
        qkv_slots = [gather_rows(part, k) for k, part in enumerate(qkv_ring)]
    with jax.named_scope("gather_gains"):
        for axis in ("y", "x", "c"):
            gains = jnp.concatenate(gather_ring(gains, axis), axis=0)
        gain_pieces = jnp.arange(devices, dtype=jnp.int32)
        gain_row = (at_z - gain_pieces % size_z) % size_z
        gain_row = gain_row * size_y + (at_y - gain_pieces // size_z % size_y) % size_y
        gain_row = gain_row * size_x + (at_x - gain_pieces // (size_z * size_y) % size_x) % size_x
        gain_row = gain_row * size_c + (
            at_c - gain_pieces // (size_z * size_y * size_x)
        ) % size_c
    with jax.named_scope("gather_output"):
        (output_own,) = after((w_output,), qkv_ring[-1])
        output_ring = gather_ring(output_own, "z")
        output_ring_sent = after(output_ring, *qkv_slots)
        output_slots = [gather_rows(part, k) for k, part in enumerate(output_ring_sent)]
    distance = jnp.arange(devices, dtype=jnp.int32)
    place = jnp.sum(
        jnp.where(gain_row[None, :] == distance[:, None], distance[None, :], 0), axis=1
    )
    gains = jnp.take(gains, place, axis=0)
    gain_onef = gains[:, 0].reshape(width)
    gain_twof = gains[:, 1].reshape(width)

    ff_width = w_gate.shape[1]
    ff_own = ff_width // size_z
    ff_rows = w_gate.shape[0]
    w_down_t = w_down.T

    def hidden_block(which):
        start = which * ff_own
        return jnp.concatenate(
            [
                lax.dynamic_slice_in_dim(w_gate, start, ff_own, axis=1),
                lax.dynamic_slice_in_dim(w_up, start, ff_own, axis=1),
                lax.dynamic_slice_in_dim(w_down_t, start, ff_own, axis=1),
            ],
            axis=1,
        )

    blocks = [hidden_block((at_z + k) % size_z) for k in range(size_z)]
    blocks = after(blocks, gains_z)
    with jax.named_scope("gather_ffn"):
        blocks = [shift(b, "z", k) if k else b for k, b in enumerate(blocks)]
    xfloat = tokens.reshape(token_rows, width).astype(F32)
    inv_one = lax.rsqrt(jnp.mean(xfloat * xfloat, axis=-1, keepdims=True) + EPS_NORM)
    normed_one = xfloat * inv_one
    hidden_first = (normed_one * gain_onef).astype(BF16)
    hidden_by_distance = by_distance(hidden_first)
    qkv = rows_product(hidden_by_distance, qkv_slots)
    query_rows = qkv[:, :query_width].reshape(
        local_sequence, context_rows, QUERY_HEADS, HEAD_WIDTH
    )
    unrotated_key = qkv[:, query_width : query_width + kv_width].reshape(
        local_sequence, context_rows, KEY_VALUE_HEADS, HEAD_WIDTH
    )
    value_own = (
        qkv[:, query_width + kv_width :].astype(BF16).reshape(local_sequence, context_rows, kv_width)
    )
    cosine_table, sine_table = rope_tables(positions, HEAD_WIDTH // 2)
    rotated_query = (
        apply_rotation(query_rows, cosine_table, sine_table)
        .astype(BF16)
        .reshape(local_sequence, context_rows, KEY_VALUE_HEADS, query_groups, HEAD_WIDTH)
    )
    rkey_own = (
        apply_rotation(unrotated_key, cosine_table, sine_table)
        .astype(BF16)
        .reshape(local_sequence, context_rows, kv_width)
    )

    def gather_sequence(value):
        value = jnp.concatenate(gather_ring(value, "x"), axis=1)
        return jnp.concatenate(gather_ring(value, "c"), axis=1)

    at_ctx = at_x * size_c + at_c
    query_index = at_ctx * context_rows + jnp.arange(context_rows, dtype=jnp.int32)
    slot = jnp.arange(count_ctx, dtype=jnp.int32)
    slot_ctx = ((at_x - slot % size_x) % size_x) * size_c + (at_c - slot // size_x) % size_c
    key_index = (
        slot_ctx[:, None] * context_rows + jnp.arange(context_rows, dtype=jnp.int32)[None, :]
    ).reshape(-1)
    segments_all = gather_sequence(segment_ids)
    allowed = (segment_ids[:, :, None] == segments_all[:, None, :]) & (
        key_index[None, None, :] <= query_index[None, :, None]
    )
    allowed = allowed[:, None, None]
    gathered = gather_sequence(jnp.concatenate([rkey_own, value_own], axis=-1))
    ffn = jnp.zeros((width, 3 * ff_own), BF16)
    blocks = after(blocks, gathered)
    for step, block in enumerate(blocks):
        with jax.named_scope("gather_ffn"):
            block_y = gather_ring(block, "y")
        for k, piece_y in enumerate(block_y):
            row = ((at_z - step) % size_z) * size_y + (at_y - k) % size_y
            ffn = lax.dynamic_update_slice_in_dim(ffn, piece_y, row * ff_rows, axis=0)
    gate_up_weight = ffn[:, : 2 * ff_own]
    down_weight_t = ffn[:, 2 * ff_own :]

    gathered_keys = gathered[..., :kv_width].reshape(
        local_sequence, sequence_length, KEY_VALUE_HEADS, HEAD_WIDTH
    )
    gathered_values = gathered[..., kv_width:].reshape(
        local_sequence, sequence_length, KEY_VALUE_HEADS, HEAD_WIDTH
    )
    scores = (
        jnp.einsum("schgd,slhd->shgcl", rotated_query, gathered_keys, preferred_element_type=F32)
        * factor
    )
    masked = jnp.where(allowed, scores, MASKED)
    expo = jnp.exp(masked)
    total = jnp.sum(expo, axis=-1, keepdims=True)
    lse = jnp.log(total)
    probs = (expo / total).astype(BF16)
    attended = jnp.einsum("shgcl,slhd->schgd", probs, gathered_values, preferred_element_type=F32)
    attended = attended.astype(BF16).reshape(token_rows, query_width)
    (cot_own,) = after((cotangent.reshape(token_rows, width),), attended)
    with jax.named_scope("gather_cot"):
        cot_slots = gather_tokens(cot_own)
    attended_by_distance = by_distance(attended)
    resid = xfloat + rows_product(attended_by_distance, output_slots)
    inv_two = lax.rsqrt(jnp.mean(resid * resid, axis=-1, keepdims=True) + EPS_NORM)
    normed_two = resid * inv_two
    h_two = (normed_two * gain_twof).astype(BF16)

    with jax.named_scope("gather_h"):
        h_slots = gather_tokens(h_two)
    hidden_slots, d_slots, d_h_slots = [], [], []
    for h_slot, cot_slot in zip(h_slots, cot_slots):
        gate_up = jnp.dot(h_slot, gate_up_weight, preferred_element_type=F32)
        gate, up_proj = gate_up[:, :ff_own], gate_up[:, ff_own:]
        sigma = jax.nn.sigmoid(gate)
        hidden = (gate * sigma * up_proj).astype(BF16)
        d_hidden = jnp.dot(cot_slot, down_weight_t, preferred_element_type=F32)
        d_up = (d_hidden * gate * sigma).astype(BF16)
        d_gate = (d_hidden * up_proj * sigma * (1.0 + gate * (1.0 - sigma))).astype(BF16)
        d_both = jnp.concatenate([d_gate, d_up], axis=1)
        d_h_slots.append(dot_t(d_both, gate_up_weight).astype(BF16))
        hidden_slots.append(hidden)
        d_slots.append(d_both)
    with jax.named_scope("reduce_dh"):
        d_h_sum = reduce_ring(reduce_locally(d_h_slots), "z")
    hidden_all = jnp.concatenate(hidden_slots, axis=0)
    h_all = jnp.concatenate(h_slots, axis=0)
    d_all = jnp.concatenate(d_slots, axis=0)
    cot_all = jnp.concatenate(cot_slots, axis=0)
    grad_ffn = [
        tdot(h_all, d_all[:, :ff_own]).astype(BF16),
        tdot(h_all, d_all[:, ff_own:]).astype(BF16),
        tdot(cot_all, hidden_all).astype(BF16),
    ]
    out = dot_t(hidden_all, down_weight_t).astype(BF16)
    (d_h_sum,), grad_ffn, out = lax.optimization_barrier(((d_h_sum,), grad_ffn, out))
    d_h_two = d_h_sum.astype(F32)

    with jax.named_scope("reduce_out"):
        out = out.reshape(size_z, -1, width)
        out_cores = reduce_axes(out, ("c",))
        out_across = reduce_axes(out_cores, ("x",))
        ffn_out = reduce_ring([out_across[k] for k in range(size_z)], "z").astype(F32)
    mixed = (resid + ffn_out).astype(BF16)
    pairs_y = []
    for k in range(size_y):
        rows_y = []
        for step in range(size_z):
            row = ((at_z - step) % size_z) * size_y + (at_y - k) % size_y
            rows_y.append(
                jnp.concatenate(
                    [
                        lax.dynamic_slice_in_dim(part, row * ff_rows, ff_rows, axis=0)
                        for part in grad_ffn
                    ],
                    axis=1,
                )
            )
        pairs_y.append(rows_y)
    with jax.named_scope("reduce_ffn"):
        ffn_own = [
            reduce_ring([pairs_y[k][step] for k in range(size_y)], "y") for step in range(size_z)
        ]

    gain_term_two = jnp.sum(d_h_two * normed_two, axis=0)
    cot_rows = cotangent.reshape(token_rows, width)
    d_resid = cot_rows.astype(F32) + norm_back(d_h_two, normed_two, inv_two, gain_twof)
    residual_gradient_second = d_resid.astype(BF16)
    attended_gradient = by_feature(
        jnp.concatenate([dot_t(residual_gradient_second, part) for part in output_slots], axis=1)
    ).astype(BF16)
    attended_gradient = attended_gradient.reshape(
        local_sequence, context_rows, KEY_VALUE_HEADS, query_groups, HEAD_WIDTH
    )
    (attended_gradient,) = after((attended_gradient,), out_cores)
    with jax.named_scope("reduce_output"):
        part = tdot(attended_by_distance, residual_gradient_second).astype(BF16)
        part_cores = reduce_axes(part.reshape(size_z, -1, width), ("c",))
        part_even = reduce_axes(part_cores[0::2], ("x", "y"))
        part_odd = reduce_axes(part_cores[1::2], ("y", "x"))
        local = [(part_odd if k % 2 else part_even)[k // 2] for k in range(size_z)]
        grad_output = reduce_ring(local, "z").astype(F32)
    probs_f = jnp.where(allowed, jnp.exp(masked - lse), 0.0)
    d_probs = jnp.einsum(
        "schgd,slhd->shgcl", attended_gradient, gathered_values, preferred_element_type=F32
    )
    delta = jnp.sum(probs_f * d_probs, axis=-1, keepdims=True)
    d_scores_b = (probs_f * (d_probs - delta) * factor).astype(BF16)
    value_gradient_local = jnp.einsum(
        "shgcl,schgd->slhd",
        probs_f.astype(BF16),
        attended_gradient,
        preferred_element_type=F32,
    )
    d_rquery = jnp.einsum(
        "shgcl,slhd->schgd", d_scores_b, gathered_keys, preferred_element_type=F32
    )
    rotated_key_gradient = jnp.einsum(
        "shgcl,schgd->slhd", d_scores_b, rotated_query, preferred_element_type=F32
    )
    kv_gradient = jnp.concatenate(
        [
            rotated_key_gradient.reshape(local_sequence, sequence_length, kv_width).astype(BF16),
            value_gradient_local.reshape(local_sequence, sequence_length, kv_width).astype(BF16),
        ],
        axis=-1,
    )
    ffn_own = after(ffn_own, kv_gradient)
    with jax.named_scope("reduce_ffn"):
        ffn_sums = [shift(b, "z", -step) if step else b for step, b in enumerate(ffn_own)]
    (kv_gradient,) = after((kv_gradient,), part_cores)
    with jax.named_scope("reduce_kv"):
        for axis in ("c", "x"):
            count = lax.axis_size(axis)
            kv_gradient = reduce_ring(jnp.split(kv_gradient, count, axis=1), axis)
    kv_gradient = kv_gradient.astype(F32)
    dquery = (
        reverse_rotation(
            d_rquery.reshape(local_sequence, context_rows, QUERY_HEADS, HEAD_WIDTH),
            cosine_table,
            sine_table,
        )
        .astype(BF16)
        .reshape(token_rows, query_width)
    )
    dkey = (
        reverse_rotation(
            kv_gradient[..., :kv_width].reshape(
                local_sequence, context_rows, KEY_VALUE_HEADS, HEAD_WIDTH
            ),
            cosine_table,
            sine_table,
        )
        .astype(BF16)
        .reshape(token_rows, kv_width)
    )
    dvalue = kv_gradient[..., kv_width:].astype(BF16).reshape(token_rows, kv_width)
    d_qkv = jnp.concatenate([dquery, dkey, dvalue], axis=1)
    (d_qkv,) = after((d_qkv,), part_even, part_odd)
    with jax.named_scope("reduce_qkv"):
        grad_qkv, local = reduce_weight(hidden_by_distance, d_qkv)
        grad_qkv = grad_qkv.astype(F32)
    ffn_sums = after(ffn_sums, local[2 % size_z])
    grad_gate = jnp.zeros((ff_rows, ff_width), F32)
    grad_up = jnp.zeros((ff_rows, ff_width), F32)
    grad_down_t = jnp.zeros((ff_rows, ff_width), F32)
    for step, block in enumerate(ffn_sums):
        start = ((at_z + step) % size_z) * ff_own
        block = block.astype(F32)
        grad_gate = lax.dynamic_update_slice_in_dim(grad_gate, block[:, :ff_own], start, axis=1)
        grad_up = lax.dynamic_update_slice_in_dim(
            grad_up, block[:, ff_own : 2 * ff_own], start, axis=1
        )
        grad_down_t = lax.dynamic_update_slice_in_dim(
            grad_down_t, block[:, 2 * ff_own :], start, axis=1
        )
    grad_down = grad_down_t.T
    d_h_one = by_feature(jnp.concatenate([dot_t(d_qkv, part) for part in qkv_slots], axis=1))
    gain_term_one = jnp.sum(d_h_one * normed_one, axis=0)
    grad_tokens = d_resid + norm_back(d_h_one, normed_one, inv_one, gain_onef)
    gain_terms = jnp.stack(
        [gain_term_one.reshape(devices, own_rows), gain_term_two.reshape(devices, own_rows)], axis=1
    )
    (gain_terms,) = after((gain_terms,), local[1 % size_z])
    gain_grads = reduce_small(jnp.take(gain_terms, gain_row, axis=0))[0]
    return (
        mixed.reshape(local_sequence, context_rows, width),
        grad_tokens.reshape(local_sequence, context_rows, width),
        gain_grads[0],
        grad_qkv[:, :query_width],
        grad_qkv[:, query_width : query_width + kv_width],
        grad_qkv[:, query_width + kv_width :],
        grad_output,
        gain_grads[1],
        grad_gate,
        grad_up,
        grad_down,
    )


def solution(mesh):
    count_dp, count_ctx = mesh.devices.shape
    along_z = 4 if count_dp % 4 == 0 else count_dp
    along_x = 2 if count_ctx % 2 == 0 else 1
    fine = Mesh(
        mesh.devices.reshape(along_z, count_dp // along_z, along_x, count_ctx // along_x),
        ("z", "y", "x", "c"),
    )
    dp, ctx, both = ("z", "y"), ("x", "c"), ("z", "y", "x", "c")
    return jax.shard_map(
        body,
        mesh=fine,
        in_specs=(
            P(dp, ctx, None),
            P(dp, ctx),
            P(dp, ctx),
            P(both),
            P(both, None),
            P(both, None),
            P(both, None),
            P(both, None),
            P(both),
            P(dp, ctx),
            P(dp, ctx),
            P(ctx, dp),
            P(dp, ctx, None),
        ),
        out_specs=(
            P(dp, ctx, None),
            P(dp, ctx, None),
            P(both),
            P(both, None),
            P(both, None),
            P(both, None),
            P(both, None),
            P(both),
            P(dp, ctx),
            P(dp, ctx),
            P(ctx, dp),
        ),
        check_vma=False,
    )
```

```python
import jax
import jax.numpy as jnp
from jax import lax
from jax.sharding import Mesh
from jax.sharding import PartitionSpec as P


QUERY_HEADS = 32
KEY_VALUE_HEADS = 8
HEAD_WIDTH = 64


EPS_NORM = 1e-05
ROPE_BASE = 500000.0
MASKED = -1e30


F32 = jnp.float32
BF16 = jnp.bfloat16


def rope_tables(where_pos, half_width):
    freqs = ROPE_BASE ** (-(jnp.arange(half_width, dtype=jnp.float32) / half_width))
    angles = where_pos.astype(jnp.float32)[..., None] * freqs
    return (jnp.cos(angles), jnp.sin(angles))


def apply_rotation(values, cosine_table, sine_table):
    half_width = values.shape[-1] // 2
    first = values[..., :half_width]
    second = values[..., half_width:]
    cosine_table = cosine_table[..., None, :]
    sine_table = sine_table[..., None, :]
    return jnp.concatenate(
        [first * cosine_table - second * sine_table, second * cosine_table + first * sine_table],
        axis=-1,
    )


def reverse_rotation(grads, cosine_table, sine_table):
    half_width = grads.shape[-1] // 2
    first = grads[..., :half_width]
    second = grads[..., half_width:]
    cosine_table = cosine_table[..., None, :]
    sine_table = sine_table[..., None, :]
    return jnp.concatenate(
        [first * cosine_table + second * sine_table, second * cosine_table - first * sine_table],
        axis=-1,
    )


def norm_back(upstream, normed, inverse, gain):
    scaled = upstream * gain
    return inverse * (scaled - normed * jnp.mean(scaled * normed, axis=-1, keepdims=True))


def tdot(left, right):
    return lax.dot_general(
        left, right, (((0,), (0,)), ((), ())), preferred_element_type=jnp.float32
    )


def dot_t(left, right):
    return lax.dot_general(
        left, right, (((1,), (1,)), ((), ())), preferred_element_type=jnp.float32
    )


def back(at, step, count):
    return lax.rem(at + (count - step % count), jnp.int32(count))


def ahead(at, step, count):
    return lax.rem(at + step, jnp.int32(count))


def shift(value, axis, step=1):
    count = lax.axis_size(axis)
    return lax.ppermute(value, axis, [(i, (i + step) % count) for i in range(count)])


def gather_ring(value, axis):
    slots = [value]
    for _ in range(lax.axis_size(axis) - 1):
        slots.append(shift(slots[-1], axis))
    return slots


def add_rounded(left, right):
    return (left.astype(F32) + right.astype(F32)).astype(left.dtype)


def reduce_ring(parts, axis):
    count = lax.axis_size(axis)
    if count == 1:
        return parts[0]
    total = parts[1]
    for k in range(2, count):
        total = add_rounded(shift(total, axis), parts[k])
    return add_rounded(shift(total, axis), parts[0])


def gather_tokens(value):
    slots = []
    for piece in gather_ring(value, "z"):
        pair = jnp.concatenate(gather_ring(piece, "x"), axis=0)
        slots.append(jnp.concatenate(gather_ring(pair, "c"), axis=0))
    return slots


def reduce_block(block):
    cores = lax.axis_size("c")
    across = lax.axis_size("x")
    rows = block.shape[0] // cores
    pair = reduce_ring([block[k * rows : (k + 1) * rows] for k in range(cores)], "c")
    rows = rows // across
    return reduce_ring([pair[k * rows : (k + 1) * rows] for k in range(across)], "x")


def reduce_locally(blocks):
    count = len(blocks)
    local = {k % count: reduce_block(blocks[k % count]) for k in range(1, count + 1)}
    return [local[k] for k in range(count)]


def hop_order(slot):
    return ("y", "x", "c") if slot % 2 == 0 else ("x", "y", "c")


def gather_rows(piece, slot):
    for axis in hop_order(slot):
        piece = jnp.concatenate(gather_ring(piece, axis), axis=0)
    return piece


def reduce_axes(block, axes):
    for axis in axes:
        rows = block.shape[-2] // lax.axis_size(axis)
        parts = [block[..., k * rows : (k + 1) * rows, :] for k in range(lax.axis_size(axis))]
        block = reduce_ring(parts, axis)
    return block


def reduce_weight(permuted, upstream):
    count = lax.axis_size("z")
    columns = permuted.shape[1] // count
    local = {}
    for step in range(1, count + 1):
        k = step % count
        part = tdot(permuted[:, k * columns : (k + 1) * columns], upstream).astype(BF16)
        local[k] = reduce_axes(part, reversed(hop_order(k)))
    local = [local[k] for k in range(count)]
    return reduce_ring(local, "z"), local


def rows_product(value, slots):
    rows = slots[0].shape[0]
    total = None
    for k, slot in enumerate(slots):
        part = jnp.dot(value[:, k * rows : (k + 1) * rows], slot, preferred_element_type=F32)
        total = part if total is None else total + part
    return total


def after(values, *waits):
    return lax.optimization_barrier((tuple(values), waits))[0]


def layer(
    tokens,
    segment_ids,
    positions,
    attn_gain,
    w_query,
    w_key,
    w_value,
    w_output,
    ffn_gain,
    w_gate,
    w_up,
    w_down,
    cotangent,
):
    everywhere = ("z", "y", "x", "c")
    size_z, size_y, size_x, size_c = (lax.axis_size(a) for a in everywhere)
    at_z, at_y, at_x, at_c = (lax.axis_index(a) for a in everywhere)
    devices = size_z * size_y * size_x * size_c
    count_ctx = size_x * size_c
    local_sequence, context_rows, width = tokens.shape
    token_rows = local_sequence * context_rows
    sequence_length = context_rows * count_ctx
    query_groups = QUERY_HEADS // KEY_VALUE_HEADS
    query_width = QUERY_HEADS * HEAD_WIDTH
    kv_width = KEY_VALUE_HEADS * HEAD_WIDTH
    factor = 1.0 / HEAD_WIDTH**0.5
    own_rows = w_query.shape[0]

    sizes = {"y": size_y, "x": size_x, "c": size_c}
    here = {"y": at_y, "x": at_x, "c": at_c}
    plane = jnp.arange(devices // size_z, dtype=jnp.int32)
    pieces = []
    for slot in range(size_z):
        stride, at = 1, {}
        for axis in hop_order(slot):
            away = (plane // stride) % sizes[axis]
            at[axis] = lax.rem(here[axis] + sizes[axis] - away, sizes[axis])
            stride *= sizes[axis]
        row = back(at_z, slot, size_z) * size_y + at["y"]
        pieces.append((row * size_x + at["x"]) * size_c + at["c"])
    piece = jnp.concatenate(pieces)
    feature = (piece[:, None] * own_rows + jnp.arange(own_rows, dtype=jnp.int32)).reshape(-1)
    selector = (jnp.arange(width, dtype=jnp.int32)[:, None] == feature[None, :]).astype(BF16)

    def by_distance(value):
        return jnp.dot(value, selector, preferred_element_type=F32).astype(BF16)

    def by_feature(value):
        return dot_t(value.astype(BF16), selector)

    lanes = 128
    qkv_width = query_width + 2 * kv_width
    gain_columns = jnp.pad(jnp.stack([attn_gain, ffn_gain], axis=1), ((0, 0), (0, lanes - 2)))
    qkv_own = jnp.concatenate([w_query, w_key, w_value, gain_columns], axis=1)
    qkv_ring = gather_ring(qkv_own, "z")
    packed_slots = [gather_rows(part, k) for k, part in enumerate(qkv_ring)]
    slot_rows = width // size_z
    qkv_slots = [part[:, :qkv_width] for part in packed_slots]
    gain_slots = [part[:, qkv_width:] for part in packed_slots]
    (output_own,) = after((w_output,), qkv_ring[-1])
    output_ring = gather_ring(output_own, "z")
    output_ring_sent = after(output_ring, *packed_slots)
    output_slots = [gather_rows(part, k) for k, part in enumerate(output_ring_sent)]
    unit = jnp.eye(slot_rows, dtype=BF16)
    gain_one_rel = jnp.concatenate([tdot(part, unit)[:1] for part in gain_slots], axis=1)
    gain_twof = sum(
        lax.dot_general(
            part,
            selector[:, k * slot_rows : (k + 1) * slot_rows],
            (((0,), (1,)), ((), ())),
            preferred_element_type=F32,
        )[1]
        for k, part in enumerate(gain_slots)
    )

    ff_width = w_gate.shape[1]
    ff_own = ff_width // size_z
    ff_rows = w_gate.shape[0]
    w_down_t = w_down.T

    def hidden_block(which):
        start = which * ff_own
        return jnp.concatenate(
            [
                lax.dynamic_slice_in_dim(w_gate, start, ff_own, axis=1),
                lax.dynamic_slice_in_dim(w_up, start, ff_own, axis=1),
                lax.dynamic_slice_in_dim(w_down_t, start, ff_own, axis=1),
            ],
            axis=1,
        )

    blocks = [hidden_block(ahead(at_z, k, size_z)) for k in range(size_z)]
    blocks = after(blocks, output_ring[-1])
    blocks = [shift(b, "z", k) if k else b for k, b in enumerate(blocks)]
    xfloat = tokens.reshape(token_rows, width).astype(F32)
    inv_one = lax.rsqrt(jnp.mean(xfloat * xfloat, axis=-1, keepdims=True) + EPS_NORM)
    normed_one = by_distance(tokens.reshape(token_rows, width)).astype(F32) * inv_one
    hidden_by_distance = (normed_one * gain_one_rel).astype(BF16)
    qkv = rows_product(hidden_by_distance, qkv_slots)
    query_rows = qkv[:, :query_width].reshape(
        local_sequence, context_rows, QUERY_HEADS, HEAD_WIDTH
    )
    unrotated_key = qkv[:, query_width : query_width + kv_width].reshape(
        local_sequence, context_rows, KEY_VALUE_HEADS, HEAD_WIDTH
    )
    value_own = (
        qkv[:, query_width + kv_width :].astype(BF16).reshape(local_sequence, context_rows, kv_width)
    )
    cosine_table, sine_table = rope_tables(positions, HEAD_WIDTH // 2)
    rotated_query = (
        apply_rotation(query_rows, cosine_table, sine_table)
        .astype(BF16)
        .reshape(local_sequence, context_rows, KEY_VALUE_HEADS, query_groups, HEAD_WIDTH)
    )
    rkey_own = (
        apply_rotation(unrotated_key, cosine_table, sine_table)
        .astype(BF16)
        .reshape(local_sequence, context_rows, kv_width)
    )

    def gather_sequence(value):
        value = jnp.concatenate(gather_ring(value, "x"), axis=1)
        return jnp.concatenate(gather_ring(value, "c"), axis=1)

    at_ctx = at_x * size_c + at_c
    query_index = at_ctx * context_rows + jnp.arange(context_rows, dtype=jnp.int32)
    slot = jnp.arange(count_ctx, dtype=jnp.int32)
    slot_ctx = ((at_x - slot % size_x) % size_x) * size_c + (at_c - slot // size_x) % size_c
    key_index = (
        slot_ctx[:, None] * context_rows + jnp.arange(context_rows, dtype=jnp.int32)[None, :]
    ).reshape(-1)
    segments_all = gather_sequence(segment_ids)
    allowed = (segment_ids[:, :, None] == segments_all[:, None, :]) & (
        key_index[None, None, :] <= query_index[None, :, None]
    )
    allowed = allowed[:, None, None]
    gathered = gather_sequence(jnp.concatenate([rkey_own, value_own], axis=-1))
    ffn = jnp.zeros((width, 3 * ff_own), BF16)
    blocks = after(blocks, gathered)
    for step, block in enumerate(blocks):
        block_y = gather_ring(block, "y")
        for k, piece_y in enumerate(block_y):
            row = back(at_z, step, size_z) * size_y + back(at_y, k, size_y)
            ffn = lax.dynamic_update_slice_in_dim(ffn, piece_y, row * ff_rows, axis=0)
    gate_up_weight = ffn[:, : 2 * ff_own]
    down_weight_t = ffn[:, 2 * ff_own :]

    gathered_keys = gathered[..., :kv_width].reshape(
        local_sequence, sequence_length, KEY_VALUE_HEADS, HEAD_WIDTH
    )
    gathered_values = gathered[..., kv_width:].reshape(
        local_sequence, sequence_length, KEY_VALUE_HEADS, HEAD_WIDTH
    )
    scores = (
        jnp.einsum("schgd,slhd->shgcl", rotated_query, gathered_keys, preferred_element_type=F32)
        * factor
    )
    masked = jnp.where(allowed, scores, MASKED)
    expo = jnp.exp(masked)
    total = jnp.sum(expo, axis=-1, keepdims=True)
    lse = jnp.log(total)
    probs = (expo / total).astype(BF16)
    attended = jnp.einsum("shgcl,slhd->schgd", probs, gathered_values, preferred_element_type=F32)
    attended = attended.astype(BF16).reshape(token_rows, query_width)
    (cot_own,) = after((cotangent.reshape(token_rows, width),), attended)
    cot_slots = gather_tokens(cot_own)
    attended_by_distance = by_distance(attended)
    resid = xfloat + rows_product(attended_by_distance, output_slots)
    inv_two = lax.rsqrt(jnp.mean(resid * resid, axis=-1, keepdims=True) + EPS_NORM)
    normed_two = resid * inv_two
    h_two = (normed_two * gain_twof).astype(BF16)

    h_slots = gather_tokens(h_two)
    d_h_slots = []
    group_rows = token_rows * size_z * count_ctx
    hidden_all = jnp.zeros((group_rows, ff_own), BF16)
    d_gate_all = jnp.zeros((group_rows, ff_own), BF16)
    d_up_all = jnp.zeros((group_rows, ff_own), BF16)
    for h_slot, cot_slot in zip(h_slots, cot_slots):
        gate_up = jnp.dot(h_slot, gate_up_weight, preferred_element_type=F32)
        gate, up_proj = gate_up[:, :ff_own], gate_up[:, ff_own:]
        sigma = jax.nn.sigmoid(gate)
        hidden = (gate * sigma * up_proj).astype(BF16)
        d_hidden = jnp.dot(cot_slot, down_weight_t, preferred_element_type=F32)
        d_up = (d_hidden * gate * sigma).astype(BF16)
        d_gate = (d_hidden * up_proj * sigma * (1.0 + gate * (1.0 - sigma))).astype(BF16)
        d_both = jnp.concatenate([d_gate, d_up], axis=1)
        d_h_slots.append(dot_t(d_both, gate_up_weight).astype(BF16))
        at_row = len(d_h_slots) * hidden.shape[0] - hidden.shape[0]
        hidden_all = lax.dynamic_update_slice(hidden_all, hidden, (at_row, 0))
        d_gate_all = lax.dynamic_update_slice(d_gate_all, d_gate, (at_row, 0))
        d_up_all = lax.dynamic_update_slice(d_up_all, d_up, (at_row, 0))
    d_h_sum = reduce_ring(reduce_locally(d_h_slots), "z")
    h_all = jnp.concatenate(h_slots, axis=0)
    cot_all = jnp.concatenate(cot_slots, axis=0)
    grad_ffn = [
        tdot(h_all, d_gate_all).astype(BF16),
        tdot(h_all, d_up_all).astype(BF16),
        tdot(cot_all, hidden_all).astype(BF16),
    ]
    out = dot_t(hidden_all, down_weight_t).astype(BF16)
    (d_h_sum,), grad_ffn, out = lax.optimization_barrier(((d_h_sum,), grad_ffn, out))
    d_h_two = d_h_sum.astype(F32)

    out = out.reshape(size_z, -1, width)
    out_cores = reduce_axes(out, ("c",))
    pairs_y = []
    for k in range(size_y):
        rows_y = []
        for step in range(size_z):
            row = back(at_z, step, size_z) * size_y + back(at_y, k, size_y)
            rows_y.append(
                jnp.concatenate(
                    [
                        lax.dynamic_slice_in_dim(part, row * ff_rows, ff_rows, axis=0)
                        for part in grad_ffn
                    ],
                    axis=1,
                )
            )
        pairs_y.append(rows_y)
    ffn_own = [
        reduce_ring([pairs_y[k][step] for k in range(size_y)], "y") for step in range(size_z)
    ]

    gain_term_two = jnp.sum(d_h_two * normed_two, axis=0)
    cot_rows = cotangent.reshape(token_rows, width)
    d_resid = cot_rows.astype(F32) + norm_back(d_h_two, normed_two, inv_two, gain_twof)
    residual_gradient_second = d_resid.astype(BF16)
    (out_cores,) = after((out_cores,), residual_gradient_second)
    early = [k for k in range(size_z) if k in (1, 2)]
    late = [k for k in range(size_z) if k not in early]
    out_early = reduce_axes(jnp.stack([out_cores[k] for k in early]), ("x",))
    attended_gradient = by_feature(
        jnp.concatenate([dot_t(residual_gradient_second, part) for part in output_slots], axis=1)
    ).astype(BF16)
    attended_gradient = attended_gradient.reshape(
        local_sequence, context_rows, KEY_VALUE_HEADS, query_groups, HEAD_WIDTH
    )
    part = tdot(attended_by_distance, residual_gradient_second).astype(BF16)
    part_cores = reduce_axes(part.reshape(size_z, -1, width), ("c",))
    probs_f = jnp.where(allowed, jnp.exp(masked - lse), 0.0)
    d_probs = jnp.einsum(
        "schgd,slhd->shgcl", attended_gradient, gathered_values, preferred_element_type=F32
    )
    delta = jnp.sum(probs_f * d_probs, axis=-1, keepdims=True)
    d_scores_b = (probs_f * (d_probs - delta) * factor).astype(BF16)
    value_gradient_local = jnp.einsum(
        "shgcl,schgd->slhd",
        probs_f.astype(BF16),
        attended_gradient,
        preferred_element_type=F32,
    )
    d_rquery = jnp.einsum(
        "shgcl,slhd->schgd", d_scores_b, gathered_keys, preferred_element_type=F32
    )
    rotated_key_gradient = jnp.einsum(
        "shgcl,schgd->slhd", d_scores_b, rotated_query, preferred_element_type=F32
    )
    kv_gradient = jnp.concatenate(
        [
            rotated_key_gradient.reshape(local_sequence, sequence_length, kv_width).astype(BF16),
            value_gradient_local.reshape(local_sequence, sequence_length, kv_width).astype(BF16),
        ],
        axis=-1,
    )
    for axis in ("c", "x"):
        count = lax.axis_size(axis)
        kv_gradient = reduce_ring(jnp.split(kv_gradient, count, axis=1), axis)
    out_cores, part_cores = after((out_cores, part_cores), kv_gradient)
    out_late = reduce_axes(jnp.stack([out_cores[k] for k in late]), ("x",))
    out_across = {k: out_early[n] for n, k in enumerate(early)}
    out_across.update({k: out_late[n] for n, k in enumerate(late)})
    ffn_out = out_across[1]
    for k in range(2, size_z):
        ffn_out = add_rounded(shift(ffn_out, "z"), out_across[k])
    ffn_own = after(ffn_own, ffn_out)
    ffn_out = shift(ffn_out, "z")
    ffn_sums = [shift(b, "z", -step) if step else b for step, b in enumerate(ffn_own)]
    part_even = reduce_axes(part_cores[0::2], ("x", "y"))
    part_odd = reduce_axes(part_cores[1::2], ("y", "x"))
    dquery = (
        reverse_rotation(
            d_rquery.reshape(local_sequence, context_rows, QUERY_HEADS, HEAD_WIDTH),
            cosine_table,
            sine_table,
        )
        .astype(BF16)
        .reshape(token_rows, query_width)
    )
    dkey = (
        reverse_rotation(
            kv_gradient[..., :kv_width].reshape(
                local_sequence, context_rows, KEY_VALUE_HEADS, HEAD_WIDTH
            ),
            cosine_table,
            sine_table,
        )
        .astype(BF16)
        .reshape(token_rows, kv_width)
    )
    dvalue = kv_gradient[..., kv_width:].astype(BF16).reshape(token_rows, kv_width)
    d_qkv = jnp.concatenate([dquery, dkey, dvalue], axis=1)
    d_h_one = jnp.concatenate([dot_t(d_qkv, part) for part in qkv_slots], axis=1)
    gain_term_one = jnp.sum(d_h_one * normed_one, axis=0, keepdims=True)

    def split(row):
        high = row.astype(BF16)
        return jnp.concatenate([high, (row - high.astype(F32)).astype(BF16)], axis=0)

    gain_rows = jnp.concatenate(
        [
            split(gain_term_one),
            by_distance(split(gain_term_two[None])),
            jnp.zeros((4, width), BF16),
        ],
        axis=0,
    )
    which = jnp.arange(8, dtype=jnp.int32)[:, None] // 2
    gain_places = (which == jnp.arange(lanes, dtype=jnp.int32)[None, :]).astype(BF16)
    left = jnp.concatenate([hidden_by_distance, gain_rows], axis=0)
    right = jnp.concatenate(
        [
            jnp.concatenate([d_qkv, jnp.zeros((token_rows, lanes), BF16)], axis=1),
            jnp.concatenate([jnp.zeros((8, qkv_width), BF16), gain_places], axis=1),
        ],
        axis=0,
    )
    grad_qkv, local = reduce_weight(left, right)
    grad_qkv = grad_qkv.astype(F32)
    part_even, part_odd = after((part_even, part_odd), local[0])
    output_local = [(part_odd if k % 2 else part_even)[k // 2] for k in range(size_z)]
    grad_output = reduce_ring(output_local, "z").astype(F32)
    (ffn_out,) = after((ffn_out,), local[0])
    mixed = (resid + add_rounded(ffn_out, out_across[0]).astype(F32)).astype(BF16)
    ffn_sums = after(ffn_sums, local[0])
    grad_gate = jnp.zeros((ff_rows, ff_width), F32)
    grad_up = jnp.zeros((ff_rows, ff_width), F32)
    grad_down_t = jnp.zeros((ff_rows, ff_width), F32)
    for step, block in enumerate(ffn_sums):
        start = ahead(at_z, step, size_z) * ff_own
        block = block.astype(F32)
        grad_gate = lax.dynamic_update_slice_in_dim(grad_gate, block[:, :ff_own], start, axis=1)
        grad_up = lax.dynamic_update_slice_in_dim(
            grad_up, block[:, ff_own : 2 * ff_own], start, axis=1
        )
        grad_down_t = lax.dynamic_update_slice_in_dim(
            grad_down_t, block[:, 2 * ff_own :], start, axis=1
        )
    grad_down = grad_down_t.T
    grad_tokens = d_resid + by_feature(norm_back(d_h_one, normed_one, inv_one, gain_one_rel))
    return (
        mixed.reshape(local_sequence, context_rows, width),
        grad_tokens.reshape(local_sequence, context_rows, width),
        grad_qkv[:, qkv_width],
        grad_qkv[:, :query_width],
        grad_qkv[:, query_width : query_width + kv_width],
        grad_qkv[:, query_width + kv_width : qkv_width],
        grad_output,
        grad_qkv[:, qkv_width + 1],
        grad_gate,
        grad_up,
        grad_down,
    )


def solution(mesh):
    count_dp, count_ctx = mesh.devices.shape
    along_z = 4 if count_dp % 4 == 0 else count_dp
    along_x = 2 if count_ctx % 2 == 0 else 1
    fine = Mesh(
        mesh.devices.reshape(along_z, count_dp // along_z, along_x, count_ctx // along_x),
        ("z", "y", "x", "c"),
    )
    dp, ctx, both = ("z", "y"), ("x", "c"), ("z", "y", "x", "c")
    return jax.shard_map(
        layer,
        mesh=fine,
        in_specs=(
            P(dp, ctx, None),
            P(dp, ctx),
            P(dp, ctx),
            P(both),
            P(both, None),
            P(both, None),
            P(both, None),
            P(both, None),
            P(both),
            P(dp, ctx),
            P(dp, ctx),
            P(ctx, dp),
            P(dp, ctx, None),
        ),
        out_specs=(
            P(dp, ctx, None),
            P(dp, ctx, None),
            P(both),
            P(both, None),
            P(both, None),
            P(both, None),
            P(both, None),
            P(both),
            P(dp, ctx),
            P(dp, ctx),
            P(ctx, dp),
        ),
        check_vma=False,
    )
```

```python
import jax
import jax.numpy as jnp
from jax import lax
from jax.sharding import Mesh
from jax.sharding import PartitionSpec as P


QUERY_HEADS = 32
KEY_VALUE_HEADS = 8
HEAD_WIDTH = 64


EPS_NORM = 1e-05
ROPE_BASE = 500000.0
MASKED = -1e30


F32 = jnp.float32
BF16 = jnp.bfloat16


def rope_tables(where_pos, half_width):
    freqs = ROPE_BASE ** (-(jnp.arange(half_width, dtype=jnp.float32) / half_width))
    angles = where_pos.astype(jnp.float32)[..., None] * freqs
    return (jnp.cos(angles), jnp.sin(angles))


def apply_rotation(values, cosine_table, sine_table):
    half_width = values.shape[-1] // 2
    first = values[..., :half_width]
    second = values[..., half_width:]
    cosine_table = cosine_table[..., None, :]
    sine_table = sine_table[..., None, :]
    return jnp.concatenate(
        [first * cosine_table - second * sine_table, second * cosine_table + first * sine_table],
        axis=-1,
    )


def reverse_rotation(grads, cosine_table, sine_table):
    half_width = grads.shape[-1] // 2
    first = grads[..., :half_width]
    second = grads[..., half_width:]
    cosine_table = cosine_table[..., None, :]
    sine_table = sine_table[..., None, :]
    return jnp.concatenate(
        [first * cosine_table + second * sine_table, second * cosine_table - first * sine_table],
        axis=-1,
    )


def norm_back(upstream, normed, inverse, gain):
    scaled = upstream * gain
    return inverse * (scaled - normed * jnp.mean(scaled * normed, axis=-1, keepdims=True))


def tdot(left, right):
    return lax.dot_general(
        left, right, (((0,), (0,)), ((), ())), preferred_element_type=jnp.float32
    )


def dot_t(left, right):
    return lax.dot_general(
        left, right, (((1,), (1,)), ((), ())), preferred_element_type=jnp.float32
    )


def back(at, step, count):
    return lax.rem(at + (count - step % count), jnp.int32(count))


def ahead(at, step, count):
    return lax.rem(at + step, jnp.int32(count))


def shift(value, axis, step=1):
    count = lax.axis_size(axis)
    return lax.ppermute(value, axis, [(i, (i + step) % count) for i in range(count)])


def gather_ring(value, axis):
    slots = [value]
    for _ in range(lax.axis_size(axis) - 1):
        slots.append(shift(slots[-1], axis))
    return slots


def add_rounded(left, right):
    return (left.astype(F32) + right.astype(F32)).astype(left.dtype)


def reduce_ring(parts, axis):
    count = lax.axis_size(axis)
    if count == 1:
        return parts[0]
    total = parts[1]
    for k in range(2, count):
        total = add_rounded(shift(total, axis), parts[k])
    return add_rounded(shift(total, axis), parts[0])


def gather_tokens(value):
    slots = []
    for piece in gather_ring(value, "z"):
        pair = jnp.concatenate(gather_ring(piece, "x"), axis=0)
        slots.append(jnp.concatenate(gather_ring(pair, "c"), axis=0))
    return slots


def reduce_block(block):
    cores = lax.axis_size("c")
    across = lax.axis_size("x")
    rows = block.shape[0] // cores
    pair = reduce_ring([block[k * rows : (k + 1) * rows] for k in range(cores)], "c")
    rows = rows // across
    return reduce_ring([pair[k * rows : (k + 1) * rows] for k in range(across)], "x")


def reduce_locally(blocks):
    count = len(blocks)
    local = {k % count: reduce_block(blocks[k % count]) for k in range(1, count + 1)}
    return [local[k] for k in range(count)]


def hop_order(slot):
    return ("y", "x", "c") if slot % 2 == 0 else ("x", "y", "c")


def gather_rows(piece, slot):
    for axis in hop_order(slot):
        piece = jnp.concatenate(gather_ring(piece, axis), axis=0)
    return piece


def reduce_axes(block, axes):
    for axis in axes:
        rows = block.shape[-2] // lax.axis_size(axis)
        parts = [block[..., k * rows : (k + 1) * rows, :] for k in range(lax.axis_size(axis))]
        block = reduce_ring(parts, axis)
    return block


def reduce_weight(permuted, upstream):
    count = lax.axis_size("z")
    columns = permuted.shape[1] // count
    local = {}
    for step in range(1, count + 1):
        k = step % count
        part = tdot(permuted[:, k * columns : (k + 1) * columns], upstream).astype(BF16)
        axes = hop_order(k)[::-1]
        part = reduce_axes(part, axes[:1])
        part = reduce_axes(part, axes[1:2])
        local[k] = reduce_axes(part, axes[2:])
    local = [local[k] for k in range(count)]
    return reduce_ring(local, "z"), local


def rows_product(value, slots):
    rows = slots[0].shape[0]
    total = None
    for k, slot in enumerate(slots):
        part = jnp.dot(value[:, k * rows : (k + 1) * rows], slot, preferred_element_type=F32)
        total = part if total is None else total + part
    return total


def after(values, *waits):
    return lax.optimization_barrier((tuple(values), waits))[0]


def layer(
    tokens,
    segment_ids,
    positions,
    attn_gain,
    w_query,
    w_key,
    w_value,
    w_output,
    ffn_gain,
    w_gate,
    w_up,
    w_down,
    cotangent,
):
    everywhere = ("z", "y", "x", "c")
    size_z, size_y, size_x, size_c = (lax.axis_size(a) for a in everywhere)
    at_z, at_y, at_x, at_c = (lax.axis_index(a) for a in everywhere)
    devices = size_z * size_y * size_x * size_c
    count_ctx = size_x * size_c
    local_sequence, context_rows, width = tokens.shape
    token_rows = local_sequence * context_rows
    sequence_length = context_rows * count_ctx
    query_groups = QUERY_HEADS // KEY_VALUE_HEADS
    query_width = QUERY_HEADS * HEAD_WIDTH
    kv_width = KEY_VALUE_HEADS * HEAD_WIDTH
    factor = 1.0 / HEAD_WIDTH**0.5
    own_rows = w_query.shape[0]

    lanes = 128
    qkv_width = query_width + 2 * kv_width
    gain_columns = jnp.pad(jnp.stack([attn_gain, ffn_gain], axis=1), ((0, 0), (0, lanes - 2)))
    qkv_own = jnp.concatenate([w_query, w_key, w_value, gain_columns], axis=1)
    qkv_ring = gather_ring(qkv_own, "z")
    qkv_last = qkv_ring[-1]
    tokens, positions, segment_ids = after(
        (tokens, positions, segment_ids), qkv_ring[2 % size_z]
    )
    w_gate, w_up, w_down = after((w_gate, w_up, w_down), qkv_last)

    sizes = {"y": size_y, "x": size_x, "c": size_c}
    here = {"y": at_y, "x": at_x, "c": at_c}
    plane = jnp.arange(devices // size_z, dtype=jnp.int32)
    pieces = []
    for slot in range(size_z):
        stride, at = 1, {}
        for axis in hop_order(slot):
            away = (plane // stride) % sizes[axis]
            at[axis] = lax.rem(here[axis] + sizes[axis] - away, sizes[axis])
            stride *= sizes[axis]
        row = back(at_z, slot, size_z) * size_y + at["y"]
        pieces.append((row * size_x + at["x"]) * size_c + at["c"])
    (piece,) = after((jnp.concatenate(pieces),), qkv_ring[1 % size_z])
    feature = (piece[:, None] * own_rows + jnp.arange(own_rows, dtype=jnp.int32)).reshape(-1)
    selector = (jnp.arange(width, dtype=jnp.int32)[:, None] == feature[None, :]).astype(BF16)

    def by_distance(value):
        return jnp.dot(value, selector, preferred_element_type=F32).astype(BF16)

    def by_feature(value):
        return dot_t(value.astype(BF16), selector)

    packed_slots = [gather_rows(part, k) for k, part in enumerate(qkv_ring)]
    slot_rows = width // size_z
    qkv_slots = [part[:, :qkv_width] for part in packed_slots]
    gain_slots = [part[:, qkv_width:] for part in packed_slots]
    (output_own,) = after((w_output,), qkv_ring[-1])
    output_ring = gather_ring(output_own, "z")
    output_ring_sent = after(output_ring, *packed_slots)
    output_slots = [gather_rows(part, k) for k, part in enumerate(output_ring_sent)]
    unit = jnp.eye(slot_rows, dtype=BF16)
    gain_one_rel = jnp.concatenate([tdot(part, unit)[:1] for part in gain_slots], axis=1)
    gain_twof = sum(
        lax.dot_general(
            part,
            selector[:, k * slot_rows : (k + 1) * slot_rows],
            (((0,), (1,)), ((), ())),
            preferred_element_type=F32,
        )[1]
        for k, part in enumerate(gain_slots)
    )

    ff_width = w_gate.shape[1]
    ff_own = ff_width // size_z
    ff_rows = w_gate.shape[0]
    w_down_t = w_down.T

    def hidden_block(which):
        start = which * ff_own
        return jnp.concatenate(
            [
                lax.dynamic_slice_in_dim(w_gate, start, ff_own, axis=1),
                lax.dynamic_slice_in_dim(w_up, start, ff_own, axis=1),
                lax.dynamic_slice_in_dim(w_down_t, start, ff_own, axis=1),
            ],
            axis=1,
        )

    blocks = [hidden_block(ahead(at_z, k, size_z)) for k in range(size_z)]
    blocks = after(blocks, output_ring[-1])
    blocks = [shift(b, "z", k) if k else b for k, b in enumerate(blocks)]
    xfloat = tokens.reshape(token_rows, width).astype(F32)
    inv_one = lax.rsqrt(jnp.mean(xfloat * xfloat, axis=-1, keepdims=True) + EPS_NORM)
    normed_one = by_distance(tokens.reshape(token_rows, width)).astype(F32) * inv_one
    hidden_by_distance = (normed_one * gain_one_rel).astype(BF16)
    qkv = rows_product(hidden_by_distance, qkv_slots)
    query_rows = qkv[:, :query_width].reshape(
        local_sequence, context_rows, QUERY_HEADS, HEAD_WIDTH
    )
    unrotated_key = qkv[:, query_width : query_width + kv_width].reshape(
        local_sequence, context_rows, KEY_VALUE_HEADS, HEAD_WIDTH
    )
    value_own = (
        qkv[:, query_width + kv_width :].astype(BF16).reshape(local_sequence, context_rows, kv_width)
    )
    cosine_table, sine_table = rope_tables(positions, HEAD_WIDTH // 2)
    rotated_query = (
        apply_rotation(query_rows, cosine_table, sine_table)
        .astype(BF16)
        .reshape(local_sequence, context_rows, KEY_VALUE_HEADS, query_groups, HEAD_WIDTH)
    )
    rkey_own = (
        apply_rotation(unrotated_key, cosine_table, sine_table)
        .astype(BF16)
        .reshape(local_sequence, context_rows, kv_width)
    )

    def gather_sequence(value):
        value = jnp.concatenate(gather_ring(value, "x"), axis=1)
        return jnp.concatenate(gather_ring(value, "c"), axis=1)

    at_ctx = at_x * size_c + at_c
    query_index = at_ctx * context_rows + jnp.arange(context_rows, dtype=jnp.int32)
    slot = jnp.arange(count_ctx, dtype=jnp.int32)
    slot_ctx = ((at_x - slot % size_x) % size_x) * size_c + (at_c - slot // size_x) % size_c
    key_index = (
        slot_ctx[:, None] * context_rows + jnp.arange(context_rows, dtype=jnp.int32)[None, :]
    ).reshape(-1)
    segments_all = gather_sequence(segment_ids)
    allowed = (segment_ids[:, :, None] == segments_all[:, None, :]) & (
        key_index[None, None, :] <= query_index[None, :, None]
    )
    allowed = allowed[:, None, None]
    gathered = gather_sequence(jnp.concatenate([rkey_own, value_own], axis=-1))
    ffn = jnp.zeros((width, 3 * ff_own), BF16)
    blocks = after(blocks, gathered)
    for step, block in enumerate(blocks):
        block_y = gather_ring(block, "y")
        for k, piece_y in enumerate(block_y):
            row = back(at_z, step, size_z) * size_y + back(at_y, k, size_y)
            ffn = lax.dynamic_update_slice_in_dim(ffn, piece_y, row * ff_rows, axis=0)
    gate_up_weight = ffn[:, : 2 * ff_own]
    down_weight_t = ffn[:, 2 * ff_own :]

    gathered_keys = gathered[..., :kv_width].reshape(
        local_sequence, sequence_length, KEY_VALUE_HEADS, HEAD_WIDTH
    )
    gathered_values = gathered[..., kv_width:].reshape(
        local_sequence, sequence_length, KEY_VALUE_HEADS, HEAD_WIDTH
    )
    scores = (
        jnp.einsum("schgd,slhd->shgcl", rotated_query, gathered_keys, preferred_element_type=F32)
        * factor
    )
    masked = jnp.where(allowed, scores, MASKED)
    expo = jnp.exp(masked)
    total = jnp.sum(expo, axis=-1, keepdims=True)
    lse = jnp.log(total)
    probs = (expo / total).astype(BF16)
    attended = jnp.einsum("shgcl,slhd->schgd", probs, gathered_values, preferred_element_type=F32)
    attended = attended.astype(BF16).reshape(token_rows, query_width)
    (cot_own,) = after((cotangent.reshape(token_rows, width),), attended)
    cot_slots = gather_tokens(cot_own)
    attended_by_distance = by_distance(attended)
    resid = xfloat + rows_product(attended_by_distance, output_slots)
    inv_two = lax.rsqrt(jnp.mean(resid * resid, axis=-1, keepdims=True) + EPS_NORM)
    normed_two = resid * inv_two
    h_two = (normed_two * gain_twof).astype(BF16)

    h_slots = gather_tokens(h_two)
    d_h_slots = []
    group_rows = token_rows * size_z * count_ctx
    hidden_all = jnp.zeros((group_rows, ff_own), BF16)
    d_gate_all = jnp.zeros((group_rows, ff_own), BF16)
    d_up_all = jnp.zeros((group_rows, ff_own), BF16)
    for h_slot, cot_slot in zip(h_slots, cot_slots):
        gate_up = jnp.dot(h_slot, gate_up_weight, preferred_element_type=F32)
        gate, up_proj = gate_up[:, :ff_own], gate_up[:, ff_own:]
        sigma = jax.nn.sigmoid(gate)
        hidden = (gate * sigma * up_proj).astype(BF16)
        d_hidden = jnp.dot(cot_slot, down_weight_t, preferred_element_type=F32)
        d_up = (d_hidden * gate * sigma).astype(BF16)
        d_gate = (d_hidden * up_proj * sigma * (1.0 + gate * (1.0 - sigma))).astype(BF16)
        d_both = jnp.concatenate([d_gate, d_up], axis=1)
        d_h_slots.append(dot_t(d_both, gate_up_weight).astype(BF16))
        at_row = len(d_h_slots) * hidden.shape[0] - hidden.shape[0]
        hidden_all = lax.dynamic_update_slice(hidden_all, hidden, (at_row, 0))
        d_gate_all = lax.dynamic_update_slice(d_gate_all, d_gate, (at_row, 0))
        d_up_all = lax.dynamic_update_slice(d_up_all, d_up, (at_row, 0))
    d_h_sum = reduce_ring(reduce_locally(d_h_slots), "z")
    h_all = jnp.concatenate(h_slots, axis=0)
    cot_all = jnp.concatenate(cot_slots, axis=0)
    grad_ffn = [
        tdot(h_all, d_gate_all).astype(BF16),
        tdot(h_all, d_up_all).astype(BF16),
        tdot(cot_all, hidden_all).astype(BF16),
    ]
    out = dot_t(hidden_all, down_weight_t).astype(BF16)
    (d_h_sum,), grad_ffn, out = lax.optimization_barrier(((d_h_sum,), grad_ffn, out))
    d_h_two = d_h_sum.astype(F32)

    out = out.reshape(size_z, -1, width)
    out_cores = reduce_axes(out, ("c",))
    pairs_y = []
    for k in range(size_y):
        rows_y = []
        for step in range(size_z):
            row = back(at_z, step, size_z) * size_y + back(at_y, k, size_y)
            rows_y.append(
                jnp.concatenate(
                    [
                        lax.dynamic_slice_in_dim(part, row * ff_rows, ff_rows, axis=0)
                        for part in grad_ffn
                    ],
                    axis=1,
                )
            )
        pairs_y.append(rows_y)
    ffn_own = {}
    for step in reversed(range(size_z)):
        ffn_own[step] = reduce_ring([pairs_y[k][step] for k in range(size_y)], "y")

    gain_term_two = jnp.sum(d_h_two * normed_two, axis=0)
    cot_rows = cotangent.reshape(token_rows, width)
    d_resid = cot_rows.astype(F32) + norm_back(d_h_two, normed_two, inv_two, gain_twof)
    residual_gradient_second = d_resid.astype(BF16)
    (out_cores,) = after((out_cores,), residual_gradient_second)
    early = [k for k in range(size_z) if k in (1, 2)]
    late = [k for k in range(size_z) if k not in early]
    out_early = reduce_axes(jnp.stack([out_cores[k] for k in early]), ("x",))
    attended_gradient = by_feature(
        jnp.concatenate([dot_t(residual_gradient_second, part) for part in output_slots], axis=1)
    ).astype(BF16)
    attended_gradient = attended_gradient.reshape(
        local_sequence, context_rows, KEY_VALUE_HEADS, query_groups, HEAD_WIDTH
    )
    part = tdot(attended_by_distance, residual_gradient_second).astype(BF16)
    part_cores = reduce_axes(part.reshape(size_z, -1, width), ("c",))
    probs_f = jnp.where(allowed, jnp.exp(masked - lse), 0.0)
    d_probs = jnp.einsum(
        "schgd,slhd->shgcl", attended_gradient, gathered_values, preferred_element_type=F32
    )
    delta = jnp.sum(probs_f * d_probs, axis=-1, keepdims=True)
    d_scores_b = (probs_f * (d_probs - delta) * factor).astype(BF16)
    value_gradient_local = jnp.einsum(
        "shgcl,schgd->slhd",
        probs_f.astype(BF16),
        attended_gradient,
        preferred_element_type=F32,
    )
    d_rquery = jnp.einsum(
        "shgcl,slhd->schgd", d_scores_b, gathered_keys, preferred_element_type=F32
    )
    rotated_key_gradient = jnp.einsum(
        "shgcl,schgd->slhd", d_scores_b, rotated_query, preferred_element_type=F32
    )
    kv_gradient = jnp.concatenate(
        [
            rotated_key_gradient.reshape(local_sequence, sequence_length, kv_width).astype(BF16),
            value_gradient_local.reshape(local_sequence, sequence_length, kv_width).astype(BF16),
        ],
        axis=-1,
    )
    steps_early = [k for k in range(size_z) if k >= 2]
    blocks_early = after([ffn_own[k] for k in steps_early], kv_gradient)
    ffn_sums = {k: shift(b, "z", -k) for k, b in zip(steps_early, blocks_early)}
    for k in range(min(2, size_z)):
        ffn_sums[k] = shift(ffn_own[k], "z", -k) if k else ffn_own[k]
    for axis in ("c", "x"):
        count = lax.axis_size(axis)
        kv_gradient = reduce_ring(jnp.split(kv_gradient, count, axis=1), axis)
    dquery = (
        reverse_rotation(
            d_rquery.reshape(local_sequence, context_rows, QUERY_HEADS, HEAD_WIDTH),
            cosine_table,
            sine_table,
        )
        .astype(BF16)
        .reshape(token_rows, query_width)
    )
    dkey = (
        reverse_rotation(
            kv_gradient[..., :kv_width].reshape(
                local_sequence, context_rows, KEY_VALUE_HEADS, HEAD_WIDTH
            ),
            cosine_table,
            sine_table,
        )
        .astype(BF16)
        .reshape(token_rows, kv_width)
    )
    dvalue = kv_gradient[..., kv_width:].astype(BF16).reshape(token_rows, kv_width)
    d_qkv = jnp.concatenate([dquery, dkey, dvalue], axis=1)
    d_h_one = jnp.concatenate([dot_t(d_qkv, part) for part in qkv_slots], axis=1)
    gain_term_one = jnp.sum(d_h_one * normed_one, axis=0, keepdims=True)

    def split(row):
        high = row.astype(BF16)
        return jnp.concatenate([high, (row - high.astype(F32)).astype(BF16)], axis=0)

    gain_rows = jnp.concatenate(
        [
            split(gain_term_one),
            by_distance(split(gain_term_two[None])),
            jnp.zeros((4, width), BF16),
        ],
        axis=0,
    )
    which = jnp.arange(8, dtype=jnp.int32)[:, None] // 2
    gain_places = (which == jnp.arange(lanes, dtype=jnp.int32)[None, :]).astype(BF16)
    left = jnp.concatenate([hidden_by_distance, gain_rows], axis=0)
    right = jnp.concatenate(
        [
            jnp.concatenate([d_qkv, jnp.zeros((token_rows, lanes), BF16)], axis=1),
            jnp.concatenate([jnp.zeros((8, qkv_width), BF16), gain_places], axis=1),
        ],
        axis=0,
    )
    grad_qkv, local = reduce_weight(left, right)
    grad_qkv = grad_qkv.astype(F32)
    (out_cores,) = after((out_cores,), local[1 % size_z])
    (part_cores,) = after((part_cores,), local[2 % size_z])
    out_late = reduce_axes(jnp.stack([out_cores[k] for k in late]), ("x",))
    out_across = {k: out_early[n] for n, k in enumerate(early)}
    out_across.update({k: out_late[n] for n, k in enumerate(late)})
    part_even = reduce_axes(part_cores[0::2], ("x", "y"))
    part_odd = reduce_axes(part_cores[1::2], ("y", "x"))
    part_even, part_odd = after((part_even, part_odd), local[0])
    output_local = [(part_odd if k % 2 else part_even)[k // 2] for k in range(size_z)]
    grad_output = reduce_ring(output_local, "z").astype(F32)
    out_local = after([out_across[k] for k in range(size_z)], local[0])
    ffn_out = reduce_ring(out_local, "z")
    mixed = (resid + ffn_out.astype(F32)).astype(BF16)
    ffn_sums = after([ffn_sums[k] for k in range(size_z)], local[0])
    grad_gate = jnp.zeros((ff_rows, ff_width), F32)
    grad_up = jnp.zeros((ff_rows, ff_width), F32)
    grad_down_t = jnp.zeros((ff_rows, ff_width), F32)
    for step, block in enumerate(ffn_sums):
        start = ahead(at_z, step, size_z) * ff_own
        grad_gate = lax.dynamic_update_slice_in_dim(
            grad_gate, block[:, :ff_own].astype(F32), start, axis=1
        )
        grad_up = lax.dynamic_update_slice_in_dim(
            grad_up, block[:, ff_own : 2 * ff_own].astype(F32), start, axis=1
        )
        grad_down_t = lax.dynamic_update_slice_in_dim(
            grad_down_t, block[:, 2 * ff_own :].astype(F32), start, axis=1
        )
    grad_down = grad_down_t.T
    grad_tokens = d_resid + by_feature(norm_back(d_h_one, normed_one, inv_one, gain_one_rel))
    return (
        mixed.reshape(local_sequence, context_rows, width),
        grad_tokens.reshape(local_sequence, context_rows, width),
        grad_qkv[:, qkv_width],
        grad_qkv[:, :query_width],
        grad_qkv[:, query_width : query_width + kv_width],
        grad_qkv[:, query_width + kv_width : qkv_width],
        grad_output,
        grad_qkv[:, qkv_width + 1],
        grad_gate,
        grad_up,
        grad_down,
    )


def solution(mesh):
    count_dp, count_ctx = mesh.devices.shape
    along_z = 4 if count_dp % 4 == 0 else count_dp
    along_x = 2 if count_ctx % 2 == 0 else 1
    fine = Mesh(
        mesh.devices.reshape(along_z, count_dp // along_z, along_x, count_ctx // along_x),
        ("z", "y", "x", "c"),
    )
    dp, ctx, both = ("z", "y"), ("x", "c"), ("z", "y", "x", "c")
    return jax.shard_map(
        layer,
        mesh=fine,
        in_specs=(
            P(dp, ctx, None),
            P(dp, ctx),
            P(dp, ctx),
            P(both),
            P(both, None),
            P(both, None),
            P(both, None),
            P(both, None),
            P(both),
            P(dp, ctx),
            P(dp, ctx),
            P(ctx, dp),
            P(dp, ctx, None),
        ),
        out_specs=(
            P(dp, ctx, None),
            P(dp, ctx, None),
            P(both),
            P(both, None),
            P(both, None),
            P(both, None),
            P(both, None),
            P(both),
            P(dp, ctx),
            P(dp, ctx),
            P(ctx, dp),
        ),
        check_vma=False,
    )
```

```python
import jax
import jax.numpy as jnp
from jax import lax
from jax.experimental import pallas as pl
from jax.experimental.pallas import tpu as pltpu
from jax.sharding import Mesh
from jax.sharding import PartitionSpec as P


QUERY_HEADS = 32
KEY_VALUE_HEADS = 8
HEAD_WIDTH = 64


EPS_NORM = 1e-05
ROPE_BASE = 500000.0
MASKED = -1e30


F32 = jnp.float32
BF16 = jnp.bfloat16


def rope_tables(where_pos, half_width):
    freqs = ROPE_BASE ** (-(jnp.arange(half_width, dtype=jnp.float32) / half_width))
    angles = where_pos.astype(jnp.float32)[..., None] * freqs
    return (jnp.cos(angles), jnp.sin(angles))


def apply_rotation(values, cosine_table, sine_table):
    half_width = values.shape[-1] // 2
    first = values[..., :half_width]
    second = values[..., half_width:]
    cosine_table = cosine_table[..., None, :]
    sine_table = sine_table[..., None, :]
    return jnp.concatenate(
        [first * cosine_table - second * sine_table, second * cosine_table + first * sine_table],
        axis=-1,
    )


def reverse_rotation(grads, cosine_table, sine_table):
    half_width = grads.shape[-1] // 2
    first = grads[..., :half_width]
    second = grads[..., half_width:]
    cosine_table = cosine_table[..., None, :]
    sine_table = sine_table[..., None, :]
    return jnp.concatenate(
        [first * cosine_table + second * sine_table, second * cosine_table - first * sine_table],
        axis=-1,
    )


def norm_back(upstream, normed, inverse, gain):
    scaled = upstream * gain
    return inverse * (scaled - normed * jnp.mean(scaled * normed, axis=-1, keepdims=True))


def tdot(left, right):
    return lax.dot_general(
        left, right, (((0,), (0,)), ((), ())), preferred_element_type=jnp.float32
    )


def dot_t(left, right):
    return lax.dot_general(
        left, right, (((1,), (1,)), ((), ())), preferred_element_type=jnp.float32
    )


def back(at, step, count):
    return lax.rem(at + (count - step % count), jnp.int32(count))


def ahead(at, step, count):
    return lax.rem(at + step, jnp.int32(count))


def shift(value, axis, step=1):
    count = lax.axis_size(axis)
    return lax.ppermute(value, axis, [(i, (i + step) % count) for i in range(count)])


def gather_ring(value, axis):
    slots = [value]
    for _ in range(lax.axis_size(axis) - 1):
        slots.append(shift(slots[-1], axis))
    return slots


def add_rounded(left, right):
    return (left.astype(F32) + right.astype(F32)).astype(left.dtype)


def reduce_ring(parts, axis):
    count = lax.axis_size(axis)
    if count == 1:
        return parts[0]
    total = parts[1]
    for k in range(2, count):
        total = add_rounded(shift(total, axis), parts[k])
    return add_rounded(shift(total, axis), parts[0])


def gather_tokens(value):
    slots = []
    for piece in gather_ring(value, "z"):
        pair = jnp.concatenate(gather_ring(piece, "x"), axis=0)
        slots.append(jnp.concatenate(gather_ring(pair, "c"), axis=0))
    return slots


def reduce_block(block):
    cores = lax.axis_size("c")
    across = lax.axis_size("x")
    rows = block.shape[0] // cores
    pair = reduce_ring([block[k * rows : (k + 1) * rows] for k in range(cores)], "c")
    rows = rows // across
    return reduce_ring([pair[k * rows : (k + 1) * rows] for k in range(across)], "x")


def reduce_locally(blocks):
    count = len(blocks)
    local = {k % count: reduce_block(blocks[k % count]) for k in range(1, count + 1)}
    return [local[k] for k in range(count)]


def hop_order(slot):
    return ("y", "x", "c") if slot % 2 == 0 else ("x", "y", "c")


def gather_rows(piece, slot):
    for axis in hop_order(slot):
        piece = jnp.concatenate(gather_ring(piece, axis), axis=0)
    return piece


def reduce_axes(block, axes):
    for axis in axes:
        rows = block.shape[-2] // lax.axis_size(axis)
        parts = [block[..., k * rows : (k + 1) * rows, :] for k in range(lax.axis_size(axis))]
        block = reduce_ring(parts, axis)
    return block


def reduce_weight(permuted, upstream):
    count = lax.axis_size("z")
    columns = permuted.shape[1] // count
    local = {}
    for step in range(1, count + 1):
        k = step % count
        part = tdot(permuted[:, k * columns : (k + 1) * columns], upstream).astype(BF16)
        axes = hop_order(k)[::-1]
        part = reduce_axes(part, axes[:1])
        part = reduce_axes(part, axes[1:2])
        local[k] = reduce_axes(part, axes[2:])
    local = [local[k] for k in range(count)]
    return reduce_ring(local, "z"), local


def rows_product(value, slots):
    rows = slots[0].shape[0]
    total = None
    for k, slot in enumerate(slots):
        part = jnp.dot(value[:, k * rows : (k + 1) * rows], slot, preferred_element_type=F32)
        total = part if total is None else total + part
    return total


def after(values, *waits):
    return lax.optimization_barrier((tuple(values), waits))[0]


def place_blocks(at_z, blocks):
    count = len(blocks)
    rows, packed = blocks[0].shape
    columns = packed // 3

    def kernel(at_ref, *refs):
        sources, (gate, up, down) = refs[:count], refs[count:]
        wanted = lax.rem(pl.program_id(0) + (count - at_ref[0]), jnp.int32(count))
        for k in range(count):

            @pl.when(wanted == k)
            def _():
                gate[...] = sources[k][:, :columns].astype(F32)
                up[...] = sources[k][:, columns : 2 * columns].astype(F32)
                down[...] = sources[k][:, 2 * columns :].astype(F32).T

    whole = pl.BlockSpec((rows, packed), lambda b, at: (0, 0))
    flat = pl.BlockSpec((rows, columns), lambda b, at: (0, b))
    tall = pl.BlockSpec((columns, rows), lambda b, at: (b, 0))
    return pl.pallas_call(
        kernel,
        grid_spec=pltpu.PrefetchScalarGridSpec(
            num_scalar_prefetch=1,
            grid=(count,),
            in_specs=[whole] * count,
            out_specs=[flat, flat, tall],
        ),
        out_shape=[
            jax.ShapeDtypeStruct((rows, columns * count), F32),
            jax.ShapeDtypeStruct((rows, columns * count), F32),
            jax.ShapeDtypeStruct((columns * count, rows), F32),
        ],
        name="place_blocks",
    )(at_z.astype(jnp.int32).reshape(1), *blocks)


def layer(
    tokens,
    segment_ids,
    positions,
    attn_gain,
    w_query,
    w_key,
    w_value,
    w_output,
    ffn_gain,
    w_gate,
    w_up,
    w_down,
    cotangent,
):
    everywhere = ("z", "y", "x", "c")
    size_z, size_y, size_x, size_c = (lax.axis_size(a) for a in everywhere)
    at_z, at_y, at_x, at_c = (lax.axis_index(a) for a in everywhere)
    devices = size_z * size_y * size_x * size_c
    count_ctx = size_x * size_c
    local_sequence, context_rows, width = tokens.shape
    token_rows = local_sequence * context_rows
    sequence_length = context_rows * count_ctx
    query_groups = QUERY_HEADS // KEY_VALUE_HEADS
    query_width = QUERY_HEADS * HEAD_WIDTH
    kv_width = KEY_VALUE_HEADS * HEAD_WIDTH
    factor = 1.0 / HEAD_WIDTH**0.5
    own_rows = w_query.shape[0]

    lanes = 128
    qkv_width = query_width + 2 * kv_width
    gain_columns = jnp.pad(jnp.stack([attn_gain, ffn_gain], axis=1), ((0, 0), (0, lanes - 2)))
    qkv_own = jnp.concatenate([w_query, w_key, w_value, gain_columns], axis=1)
    qkv_ring = gather_ring(qkv_own, "z")
    qkv_last = qkv_ring[-1]
    tokens, positions, segment_ids = after(
        (tokens, positions, segment_ids), qkv_ring[2 % size_z]
    )
    w_gate, w_up, w_down = after((w_gate, w_up, w_down), qkv_last)

    sizes = {"y": size_y, "x": size_x, "c": size_c}
    here = {"y": at_y, "x": at_x, "c": at_c}
    plane = jnp.arange(devices // size_z, dtype=jnp.int32)
    pieces = []
    for slot in range(size_z):
        stride, at = 1, {}
        for axis in hop_order(slot):
            away = (plane // stride) % sizes[axis]
            at[axis] = lax.rem(here[axis] + sizes[axis] - away, sizes[axis])
            stride *= sizes[axis]
        row = back(at_z, slot, size_z) * size_y + at["y"]
        pieces.append((row * size_x + at["x"]) * size_c + at["c"])
    (piece,) = after((jnp.concatenate(pieces),), qkv_ring[1 % size_z])
    feature = (piece[:, None] * own_rows + jnp.arange(own_rows, dtype=jnp.int32)).reshape(-1)
    selector = (jnp.arange(width, dtype=jnp.int32)[:, None] == feature[None, :]).astype(BF16)

    def by_distance(value):
        return jnp.dot(value, selector, preferred_element_type=F32).astype(BF16)

    def by_feature(value):
        return dot_t(value.astype(BF16), selector)

    packed_slots = [gather_rows(part, k) for k, part in enumerate(qkv_ring)]
    slot_rows = width // size_z
    qkv_slots = [part[:, :qkv_width] for part in packed_slots]
    gain_slots = [part[:, qkv_width:] for part in packed_slots]
    (output_own,) = after((w_output,), qkv_ring[-1])
    output_ring = gather_ring(output_own, "z")
    output_ring_sent = after(output_ring, *packed_slots)
    output_slots = [gather_rows(part, k) for k, part in enumerate(output_ring_sent)]
    unit = jnp.eye(slot_rows, dtype=BF16)
    gain_one_rel = jnp.concatenate([tdot(part, unit)[:1] for part in gain_slots], axis=1)
    gain_twof = sum(
        lax.dot_general(
            part,
            selector[:, k * slot_rows : (k + 1) * slot_rows],
            (((0,), (1,)), ((), ())),
            preferred_element_type=F32,
        )[1]
        for k, part in enumerate(gain_slots)
    )

    ff_width = w_gate.shape[1]
    ff_own = ff_width // size_z
    ff_rows = w_gate.shape[0]
    w_down_t = w_down.T

    def hidden_block(which):
        start = which * ff_own
        return jnp.concatenate(
            [
                lax.dynamic_slice_in_dim(w_gate, start, ff_own, axis=1),
                lax.dynamic_slice_in_dim(w_up, start, ff_own, axis=1),
                lax.dynamic_slice_in_dim(w_down_t, start, ff_own, axis=1),
            ],
            axis=1,
        )

    blocks = [hidden_block(ahead(at_z, k, size_z)) for k in range(size_z)]
    blocks = after(blocks, output_ring[-1])
    blocks = [shift(b, "z", k) if k else b for k, b in enumerate(blocks)]
    xfloat = tokens.reshape(token_rows, width).astype(F32)
    inv_one = lax.rsqrt(jnp.mean(xfloat * xfloat, axis=-1, keepdims=True) + EPS_NORM)
    normed_one = by_distance(tokens.reshape(token_rows, width)).astype(F32) * inv_one
    hidden_by_distance = (normed_one * gain_one_rel).astype(BF16)
    qkv = rows_product(hidden_by_distance, qkv_slots)
    query_rows = qkv[:, :query_width].reshape(
        local_sequence, context_rows, QUERY_HEADS, HEAD_WIDTH
    )
    unrotated_key = qkv[:, query_width : query_width + kv_width].reshape(
        local_sequence, context_rows, KEY_VALUE_HEADS, HEAD_WIDTH
    )
    value_own = (
        qkv[:, query_width + kv_width :].astype(BF16).reshape(local_sequence, context_rows, kv_width)
    )
    cosine_table, sine_table = rope_tables(positions, HEAD_WIDTH // 2)
    rotated_query = (
        apply_rotation(query_rows, cosine_table, sine_table)
        .astype(BF16)
        .reshape(local_sequence, context_rows, KEY_VALUE_HEADS, query_groups, HEAD_WIDTH)
    )
    rkey_own = (
        apply_rotation(unrotated_key, cosine_table, sine_table)
        .astype(BF16)
        .reshape(local_sequence, context_rows, kv_width)
    )

    def gather_sequence(value):
        value = jnp.concatenate(gather_ring(value, "x"), axis=1)
        return jnp.concatenate(gather_ring(value, "c"), axis=1)

    at_ctx = at_x * size_c + at_c
    query_index = at_ctx * context_rows + jnp.arange(context_rows, dtype=jnp.int32)
    slot = jnp.arange(count_ctx, dtype=jnp.int32)
    slot_ctx = ((at_x - slot % size_x) % size_x) * size_c + (at_c - slot // size_x) % size_c
    key_index = (
        slot_ctx[:, None] * context_rows + jnp.arange(context_rows, dtype=jnp.int32)[None, :]
    ).reshape(-1)
    segments_all = gather_sequence(segment_ids)
    allowed = (segment_ids[:, :, None] == segments_all[:, None, :]) & (
        key_index[None, None, :] <= query_index[None, :, None]
    )
    allowed = allowed[:, None, None]
    gathered = gather_sequence(jnp.concatenate([rkey_own, value_own], axis=-1))
    ffn = jnp.zeros((width, 3 * ff_own), BF16)
    blocks = after(blocks, gathered)
    for step, block in enumerate(blocks):
        block_y = gather_ring(block, "y")
        for k, piece_y in enumerate(block_y):
            row = back(at_z, step, size_z) * size_y + back(at_y, k, size_y)
            ffn = lax.dynamic_update_slice_in_dim(ffn, piece_y, row * ff_rows, axis=0)
    gate_up_weight = ffn[:, : 2 * ff_own]
    down_weight_t = ffn[:, 2 * ff_own :]

    gathered_keys = gathered[..., :kv_width].reshape(
        local_sequence, sequence_length, KEY_VALUE_HEADS, HEAD_WIDTH
    )
    gathered_values = gathered[..., kv_width:].reshape(
        local_sequence, sequence_length, KEY_VALUE_HEADS, HEAD_WIDTH
    )
    scores = (
        jnp.einsum("schgd,slhd->shgcl", rotated_query, gathered_keys, preferred_element_type=F32)
        * factor
    )
    masked = jnp.where(allowed, scores, MASKED)
    expo = jnp.exp(masked)
    total = jnp.sum(expo, axis=-1, keepdims=True)
    lse = jnp.log(total)
    probs = (expo / total).astype(BF16)
    attended = jnp.einsum("shgcl,slhd->schgd", probs, gathered_values, preferred_element_type=F32)
    attended = attended.astype(BF16).reshape(token_rows, query_width)
    (cot_own,) = after((cotangent.reshape(token_rows, width),), attended)
    cot_slots = gather_tokens(cot_own)
    attended_by_distance = by_distance(attended)
    resid = xfloat + rows_product(attended_by_distance, output_slots)
    inv_two = lax.rsqrt(jnp.mean(resid * resid, axis=-1, keepdims=True) + EPS_NORM)
    normed_two = resid * inv_two
    h_two = (normed_two * gain_twof).astype(BF16)

    h_slots = gather_tokens(h_two)
    d_h_slots = []
    group_rows = token_rows * size_z * count_ctx
    hidden_all = jnp.zeros((group_rows, ff_own), BF16)
    d_gate_all = jnp.zeros((group_rows, ff_own), BF16)
    d_up_all = jnp.zeros((group_rows, ff_own), BF16)
    for h_slot, cot_slot in zip(h_slots, cot_slots):
        gate_up = jnp.dot(h_slot, gate_up_weight, preferred_element_type=F32)
        gate, up_proj = gate_up[:, :ff_own], gate_up[:, ff_own:]
        sigma = jax.nn.sigmoid(gate)
        hidden = (gate * sigma * up_proj).astype(BF16)
        d_hidden = jnp.dot(cot_slot, down_weight_t, preferred_element_type=F32)
        d_up = (d_hidden * gate * sigma).astype(BF16)
        d_gate = (d_hidden * up_proj * sigma * (1.0 + gate * (1.0 - sigma))).astype(BF16)
        d_both = jnp.concatenate([d_gate, d_up], axis=1)
        d_h_slots.append(dot_t(d_both, gate_up_weight).astype(BF16))
        at_row = len(d_h_slots) * hidden.shape[0] - hidden.shape[0]
        hidden_all = lax.dynamic_update_slice(hidden_all, hidden, (at_row, 0))
        d_gate_all = lax.dynamic_update_slice(d_gate_all, d_gate, (at_row, 0))
        d_up_all = lax.dynamic_update_slice(d_up_all, d_up, (at_row, 0))
    d_h_sum = reduce_ring(reduce_locally(d_h_slots), "z")
    h_all = jnp.concatenate(h_slots, axis=0)
    cot_all = jnp.concatenate(cot_slots, axis=0)
    grad_ffn = [
        tdot(h_all, d_gate_all).astype(BF16),
        tdot(h_all, d_up_all).astype(BF16),
        tdot(cot_all, hidden_all).astype(BF16),
    ]
    out = dot_t(hidden_all, down_weight_t).astype(BF16)
    (d_h_sum,), grad_ffn, out = lax.optimization_barrier(((d_h_sum,), grad_ffn, out))
    d_h_two = d_h_sum.astype(F32)

    out = out.reshape(size_z, -1, width)
    out_cores = reduce_axes(out, ("c",))
    pairs_y = []
    for k in range(size_y):
        rows_y = []
        for step in range(size_z):
            row = back(at_z, step, size_z) * size_y + back(at_y, k, size_y)
            rows_y.append(
                jnp.concatenate(
                    [
                        lax.dynamic_slice_in_dim(part, row * ff_rows, ff_rows, axis=0)
                        for part in grad_ffn
                    ],
                    axis=1,
                )
            )
        pairs_y.append(rows_y)
    ffn_own = {}
    for step in reversed(range(size_z)):
        ffn_own[step] = reduce_ring([pairs_y[k][step] for k in range(size_y)], "y")

    gain_term_two = jnp.sum(d_h_two * normed_two, axis=0)
    cot_rows = cotangent.reshape(token_rows, width)
    d_resid = cot_rows.astype(F32) + norm_back(d_h_two, normed_two, inv_two, gain_twof)
    residual_gradient_second = d_resid.astype(BF16)
    (out_cores,) = after((out_cores,), residual_gradient_second)
    early = [k for k in range(size_z) if k in (1, 2)]
    late = [k for k in range(size_z) if k not in early]
    out_early = reduce_axes(jnp.stack([out_cores[k] for k in early]), ("x",))
    attended_gradient = by_feature(
        jnp.concatenate([dot_t(residual_gradient_second, part) for part in output_slots], axis=1)
    ).astype(BF16)
    attended_gradient = attended_gradient.reshape(
        local_sequence, context_rows, KEY_VALUE_HEADS, query_groups, HEAD_WIDTH
    )
    part = tdot(attended_by_distance, residual_gradient_second).astype(BF16)
    part_cores = reduce_axes(part.reshape(size_z, -1, width), ("c",))
    probs_f = jnp.where(allowed, jnp.exp(masked - lse), 0.0)
    d_probs = jnp.einsum(
        "schgd,slhd->shgcl", attended_gradient, gathered_values, preferred_element_type=F32
    )
    delta = jnp.sum(probs_f * d_probs, axis=-1, keepdims=True)
    d_scores_b = (probs_f * (d_probs - delta) * factor).astype(BF16)
    value_gradient_local = jnp.einsum(
        "shgcl,schgd->slhd",
        probs_f.astype(BF16),
        attended_gradient,
        preferred_element_type=F32,
    )
    d_rquery = jnp.einsum(
        "shgcl,slhd->schgd", d_scores_b, gathered_keys, preferred_element_type=F32
    )
    rotated_key_gradient = jnp.einsum(
        "shgcl,schgd->slhd", d_scores_b, rotated_query, preferred_element_type=F32
    )
    kv_gradient = jnp.concatenate(
        [
            rotated_key_gradient.reshape(local_sequence, sequence_length, kv_width).astype(BF16),
            value_gradient_local.reshape(local_sequence, sequence_length, kv_width).astype(BF16),
        ],
        axis=-1,
    )
    steps_early = [k for k in range(size_z) if k >= 2]
    blocks_early = after([ffn_own[k] for k in steps_early], kv_gradient)
    ffn_sums = {k: shift(b, "z", -k) for k, b in zip(steps_early, blocks_early)}
    for k in range(min(2, size_z)):
        ffn_sums[k] = shift(ffn_own[k], "z", -k) if k else ffn_own[k]
    for axis in ("c", "x"):
        count = lax.axis_size(axis)
        kv_gradient = reduce_ring(jnp.split(kv_gradient, count, axis=1), axis)
    dquery = (
        reverse_rotation(
            d_rquery.reshape(local_sequence, context_rows, QUERY_HEADS, HEAD_WIDTH),
            cosine_table,
            sine_table,
        )
        .astype(BF16)
        .reshape(token_rows, query_width)
    )
    dkey = (
        reverse_rotation(
            kv_gradient[..., :kv_width].reshape(
                local_sequence, context_rows, KEY_VALUE_HEADS, HEAD_WIDTH
            ),
            cosine_table,
            sine_table,
        )
        .astype(BF16)
        .reshape(token_rows, kv_width)
    )
    dvalue = kv_gradient[..., kv_width:].astype(BF16).reshape(token_rows, kv_width)
    d_qkv = jnp.concatenate([dquery, dkey, dvalue], axis=1)
    d_h_one = jnp.concatenate([dot_t(d_qkv, part) for part in qkv_slots], axis=1)
    gain_term_one = jnp.sum(d_h_one * normed_one, axis=0, keepdims=True)

    def split(row):
        high = row.astype(BF16)
        return jnp.concatenate([high, (row - high.astype(F32)).astype(BF16)], axis=0)

    gain_rows = jnp.concatenate(
        [
            split(gain_term_one),
            by_distance(split(gain_term_two[None])),
            jnp.zeros((4, width), BF16),
        ],
        axis=0,
    )
    which = jnp.arange(8, dtype=jnp.int32)[:, None] // 2
    gain_places = (which == jnp.arange(lanes, dtype=jnp.int32)[None, :]).astype(BF16)
    left = jnp.concatenate([hidden_by_distance, gain_rows], axis=0)
    right = jnp.concatenate(
        [
            jnp.concatenate([d_qkv, jnp.zeros((token_rows, lanes), BF16)], axis=1),
            jnp.concatenate([jnp.zeros((8, qkv_width), BF16), gain_places], axis=1),
        ],
        axis=0,
    )
    grad_qkv, local = reduce_weight(left, right)
    grad_qkv = grad_qkv.astype(F32)
    (out_cores,) = after((out_cores,), local[1 % size_z])
    (part_cores,) = after((part_cores,), local[2 % size_z])
    out_late = reduce_axes(jnp.stack([out_cores[k] for k in late]), ("x",))
    out_across = {k: out_early[n] for n, k in enumerate(early)}
    out_across.update({k: out_late[n] for n, k in enumerate(late)})
    part_even = reduce_axes(part_cores[0::2], ("x", "y"))
    part_odd = reduce_axes(part_cores[1::2], ("y", "x"))
    part_even, part_odd = after((part_even, part_odd), local[0])
    output_local = [(part_odd if k % 2 else part_even)[k // 2] for k in range(size_z)]
    grad_output = reduce_ring(output_local, "z").astype(F32)
    out_local = after([out_across[k] for k in range(size_z)], local[0])
    ffn_out = reduce_ring(out_local, "z")
    mixed = (resid + ffn_out.astype(F32)).astype(BF16)
    ffn_sums = after([ffn_sums[k] for k in range(size_z)], local[0])
    grad_gate, grad_up, grad_down = place_blocks(at_z, ffn_sums)
    grad_tokens = d_resid + by_feature(norm_back(d_h_one, normed_one, inv_one, gain_one_rel))
    return (
        mixed.reshape(local_sequence, context_rows, width),
        grad_tokens.reshape(local_sequence, context_rows, width),
        grad_qkv[:, qkv_width],
        grad_qkv[:, :query_width],
        grad_qkv[:, query_width : query_width + kv_width],
        grad_qkv[:, query_width + kv_width : qkv_width],
        grad_output,
        grad_qkv[:, qkv_width + 1],
        grad_gate,
        grad_up,
        grad_down,
    )


def solution(mesh):
    count_dp, count_ctx = mesh.devices.shape
    along_z = 4 if count_dp % 4 == 0 else count_dp
    along_x = 2 if count_ctx % 2 == 0 else 1
    fine = Mesh(
        mesh.devices.reshape(along_z, count_dp // along_z, along_x, count_ctx // along_x),
        ("z", "y", "x", "c"),
    )
    dp, ctx, both = ("z", "y"), ("x", "c"), ("z", "y", "x", "c")
    return jax.shard_map(
        layer,
        mesh=fine,
        in_specs=(
            P(dp, ctx, None),
            P(dp, ctx),
            P(dp, ctx),
            P(both),
            P(both, None),
            P(both, None),
            P(both, None),
            P(both, None),
            P(both),
            P(dp, ctx),
            P(dp, ctx),
            P(ctx, dp),
            P(dp, ctx, None),
        ),
        out_specs=(
            P(dp, ctx, None),
            P(dp, ctx, None),
            P(both),
            P(both, None),
            P(both, None),
            P(both, None),
            P(both, None),
            P(both),
            P(dp, ctx),
            P(dp, ctx),
            P(ctx, dp),
        ),
        check_vma=False,
    )
```
